32 devices in a mesh: dp: 8 (over z, core), tensor: 4 (over y, x).
Axes of the slice: x: 2, y: 2, z: 4, core: 2. Of those that a mesh axis runs over, the one named last changes fastest.
Arguments:
- tokens: bfloat16 [16384, 2048], P(('dp', 'tensor')), may hold values from -6 to 6
- cotangent: bfloat16 [16384, 2048], P(('dp', 'tensor')), may hold values from -12 to 12
- lengths: int32 [8], P('dp'), may hold values from 512 to 2048, as said below
- query_weight: bfloat16 [2048, 2048], P('dp', 'tensor'), may hold values from -0.125 to 0.125
- key_weight: bfloat16 [2048, 2048], P('dp', 'tensor'), may hold values from -0.125 to 0.125
- value_weight: bfloat16 [2048, 2048], P('dp', 'tensor'), may hold values from -0.125 to 0.125
- out_weight: bfloat16 [2048, 2048], P('dp', 'tensor'), may hold values from -3 to 3
- up_weight: bfloat16 [2048, 8192], P('dp', 'tensor'), may hold values from -0.125 to 0.125
- down_weight: bfloat16 [2048, 8192], P('dp', 'tensor'), may hold values from -0.0625 to 0.0625
- query_bias: float32 [2048], replicated, may hold values from -1.25 to 1.25
- value_bias: float32 [2048], replicated, may hold values from -0.0625 to 0.0625
- out_bias: float32 [2048], replicated, may hold values from -0.625 to 0.625
- norm1_gain: float32 [2048], replicated, may hold values from 0.5 to 1.5
- norm1_shift: float32 [2048], replicated, may hold values from -0.625 to 0.625
- up_bias: float32 [8192], replicated, may hold values from -0.625 to 0.625
- down_bias: float32 [2048], replicated, may hold values from -0.625 to 0.625
- norm2_gain: float32 [2048], replicated, may hold values from 0.5 to 1.5
- norm2_shift: float32 [2048], replicated, may hold values from -0.625 to 0.625
Outputs:
- layer_out: bfloat16 [16384, 2048], P(('dp', 'tensor'))
- tokens_grad: bfloat16 [16384, 2048], P(('dp', 'tensor'))
- query_weight_grad: float32 [2048, 2048], P('dp', 'tensor')
- key_weight_grad: float32 [2048, 2048], P('dp', 'tensor')
- value_weight_grad: float32 [2048, 2048], P('dp', 'tensor')
- out_weight_grad: float32 [2048, 2048], P('dp', 'tensor')
- up_weight_grad: float32 [2048, 8192], P('dp', 'tensor')
- down_weight_grad: float32 [2048, 8192], P('dp', 'tensor')
- query_bias_grad: float32 [2048], P(('dp', 'tensor'))
- value_bias_grad: float32 [2048], P(('dp', 'tensor'))
- out_bias_grad: float32 [2048], P(('dp', 'tensor'))
- norm1_gain_grad: float32 [2048], P(('dp', 'tensor'))
- norm1_shift_grad: float32 [2048], P(('dp', 'tensor'))
- up_bias_grad: float32 [8192], P(('dp', 'tensor'))
- down_bias_grad: float32 [2048], P(('dp', 'tensor'))
- norm2_gain_grad: float32 [2048], P(('dp', 'tensor'))
- norm2_shift_grad: float32 [2048], P(('dp', 'tensor'))
The draws below stay inside these ranges and needn't reach their ends.
Inputs may be any that keep to these rules, and one draw needn't show every extreme that they name: `lengths`: in every draw one slot holds a sequence of the full 2048 tokens.
All inputs are finite; a program needn't handle non-finite values.
Results may differ from the reference program's by a relative error of at most 0.025.
Values may be sent and summed in bfloat16 or wider, within the bound.
No kernel may reach another device: no remote copies, remote signals or barrier semaphores. Data moves between devices by JAX's collectives and lax.ppermute only.
A program may use at most 256 MiB of HBM per device.

```python
import jax
import jax.numpy as jnp
from jax import lax

D = 2048
HEADS = 16
HEAD_DIM = 128
FF = 8192
SEQ_LEN = 2048
MIN_LEN = 512
TOKENS = 16384
N_DP = 8
N_TENSOR = 4


def draw_lengths(key, part):
    first, second = jax.random.split(jax.random.fold_in(key, 7))
    drawn = jax.random.randint(first, (N_DP,), MIN_LEN, SEQ_LEN + 1)
    chosen = jax.random.randint(second, (), 0, N_DP)
    return jnp.where(jnp.arange(N_DP) == chosen, SEQ_LEN, drawn).astype(jnp.int32)


def spiked(array, rng, source, target, parts, factor):
    owner, partner = [(jnp.arange(array.shape[position]) // (array.shape[position] // parts)).reshape([-1 if axis == position else 1 for axis in range(array.ndim)]) for position in (source, target)]
    chosen = jax.random.permutation(rng, parts)[partner]
    strong = (owner == chosen) | (owner == (partner + parts // 2) % parts)
    return jnp.where(strong, factor * array, array)


def steps_of(stream_key, shape, cuts, smallest, top_value):
    level, own = 1.0, jax.random.fold_in(stream_key, 6)
    for axis_at, blocks in cuts:
        steps = jnp.exp(jax.random.uniform(jax.random.fold_in(own, axis_at), (blocks,), jnp.float32, smallest / len(cuts), top_value / len(cuts)))
        level = level * jnp.repeat(steps, shape[axis_at] // blocks).reshape([-1 if axis == axis_at else 1 for axis in range(len(shape))])
    return level


def bell_draw(key, dims, width, reach, shards=(), kind=jnp.bfloat16):
    values = jax.random.normal(key, dims, jnp.float32) * width
    if len(shards) > 0:
        values = steps_of(key, dims, shards, -0.22, 0.18) * values
    return jnp.clip(values, min=-reach, max=reach).astype(kind)


def gaussian_with(key, extent, scale, most, cuts, heavy, held_as=jnp.bfloat16):
    array = scale * jax.random.normal(key, extent, jnp.float32)
    if cuts:
        array = array * steps_of(key, extent, cuts, -0.22, 0.18)
    return jnp.clip(spiked(array, jax.random.fold_in(key, 3), *heavy), -most, most).astype(held_as)


def setup_inputs(seed: int = 0) -> dict:
    arg_keys = jax.random.split(jax.random.key(seed), 19)
    tokens = bell_draw(arg_keys[0], (TOKENS, D), 1.0, 6.0, ((0, 32),))
    cotangent = gaussian_with(arg_keys[1], (TOKENS, D), 1.0, 12.0, ((0, 32),), (0, 1, 32, 2.75))
    lengths = draw_lengths(jax.random.fold_in(arg_keys[18], 71), 0)
    query_weight = bell_draw(arg_keys[3], (D, D), D ** -0.5, 0.125, ((0, 8), (1, 4)))
    key_weight = bell_draw(arg_keys[4], (D, D), D ** -0.5, 0.125, ((0, 8), (1, 4)))
    value_weight = bell_draw(arg_keys[5], (D, D), D ** -0.5, 0.125, ((0, 8), (1, 4)))
    out_weight = bell_draw(arg_keys[6], (D, D), (max(4 * D // SEQ_LEN, 1)) ** -0.5, 3.0, ((0, 8), (1, 4)))
    up_weight = bell_draw(arg_keys[7], (D, FF), D ** -0.5, 0.125, ((0, 8), (1, 4)))
    down_weight = bell_draw(arg_keys[8], (D, FF), FF ** -0.5, 0.0625, ((0, 8), (1, 4)))
    query_bias = bell_draw(arg_keys[9], (D,), 0.2, 1.25, (), jnp.float32)
    value_bias = bell_draw(arg_keys[10], (D,), 0.01, 0.0625, (), jnp.float32)
    out_bias = bell_draw(arg_keys[11], (D,), 0.1, 0.625, (), jnp.float32)
    norm1_gain = jnp.clip(1.0 + 0.1 * jax.random.normal(arg_keys[12], (D,), jnp.float32), 0.5, 1.5)
    norm1_shift = bell_draw(arg_keys[13], (D,), 0.1, 0.625, (), jnp.float32)
    up_bias = bell_draw(arg_keys[14], (FF,), 0.1, 0.625, (), jnp.float32)
    down_bias = bell_draw(arg_keys[15], (D,), 0.1, 0.625, (), jnp.float32)
    norm2_gain = jnp.clip(1.0 + 0.1 * jax.random.normal(arg_keys[16], (D,), jnp.float32), 0.5, 1.5)
    norm2_shift = bell_draw(arg_keys[17], (D,), 0.1, 0.625, (), jnp.float32)
    return {"tokens": tokens, "cotangent": cotangent, "lengths": lengths, "query_weight": query_weight, "key_weight": key_weight, "value_weight": value_weight, "out_weight": out_weight, "up_weight": up_weight, "down_weight": down_weight, "query_bias": query_bias, "value_bias": value_bias, "out_bias": out_bias, "norm1_gain": norm1_gain, "norm1_shift": norm1_shift, "up_bias": up_bias, "down_bias": down_bias, "norm2_gain": norm2_gain, "norm2_shift": norm2_shift}


norm_eps = 1e-06
masked_score = -1e+30

@jax.custom_vjp
def low(v):
    return lax.optimization_barrier(v.astype(jnp.bfloat16)).astype(jnp.float32)

@jax.custom_vjp
def low_back(v):
    return v

def low_keep(v):
    return (low(v), None)

def low_pass(kept, grad):
    return (grad,)

def back_keep(v):
    return (v, None)

def back_low(kept, grad):
    return (low(grad),)
low.defvjp(low_keep, low_pass)
low_back.defvjp(back_keep, back_low)

def matmul(left, right):
    return jnp.dot(left, right, precision=lax.Precision.HIGHEST, preferred_element_type=jnp.float32)

def norm_rows(value, gain, shift):
    centred = value - lax.optimization_barrier(jnp.mean(value, axis=-1, keepdims=True))
    inverse = lax.rsqrt(lax.optimization_barrier(jnp.mean(centred * centred, axis=-1, keepdims=True)) + norm_eps)
    return centred * inverse * gain + shift

def smooth_gate(value):
    return jax.nn.gelu(value, approximate=True)

def layer(tokens, params, slot_len):
    query_weight, key_weight, value_weight, out_weight, up_weight, down_weight, query_bias, value_bias, out_bias, norm1_gain, norm1_shift, up_bias, down_bias, norm2_gain, norm2_shift = params
    head_cols = D // N_TENSOR
    hidden_cols = FF // N_TENSOR
    query_parts, key_parts, value_parts = ([], [], [])
    for group in range(N_TENSOR):
        lo_col = group * head_cols
        hi_col = lo_col + head_cols
        source = low_back(tokens)
        query_parts.append(low_back(low(matmul(source, query_weight[:, lo_col:hi_col]) + query_bias[lo_col:hi_col])))
        key_parts.append(low_back(low(matmul(source, key_weight[:, lo_col:hi_col]))))
        value_parts.append(low_back(low(matmul(source, value_weight[:, lo_col:hi_col]) + value_bias[lo_col:hi_col])))
    queries = jnp.concatenate(query_parts, axis=1)
    keys = jnp.concatenate(key_parts, axis=1)
    values = jnp.concatenate(value_parts, axis=1)
    block = min(512, SEQ_LEN)
    blocks = SEQ_LEN // block
    key_heads = keys.reshape(SEQ_LEN, HEADS, HEAD_DIM)
    value_heads = values.reshape(SEQ_LEN, HEADS, HEAD_DIM)
    key_live = jnp.arange(SEQ_LEN, dtype=jnp.int32) < slot_len
    scale = HEAD_DIM ** (-0.5)

    def attend(query_block):
        raw = jnp.einsum('qhd,khd->hqk', query_block, key_heads, precision=lax.Precision.HIGHEST) * scale
        scores = jnp.where(key_live, low_back(raw), masked_score)
        probs = jnp.exp(scores - jax.nn.logsumexp(scores, axis=-1, keepdims=True))
        return jnp.einsum('hqk,khd->qhd', low(probs), value_heads, precision=lax.Precision.HIGHEST)
    context = lax.map(jax.checkpoint(attend), queries.reshape(blocks, block, HEADS, HEAD_DIM))
    context = low_back(low(context.reshape(SEQ_LEN, D)))
    attn_total = jnp.zeros((SEQ_LEN, D), jnp.float32)
    for group in range(N_TENSOR):
        lo_col = group * head_cols
        hi_col = lo_col + head_cols
        attn_total = attn_total + low(matmul(context[:, lo_col:hi_col], out_weight[:, lo_col:hi_col].T))
    attn_out = low_back(attn_total)
    mid = norm_rows(tokens + attn_out + out_bias, norm1_gain, norm1_shift)
    mid_low = low(mid)
    ffn_total = jnp.zeros((SEQ_LEN, D), jnp.float32)
    for group in range(N_TENSOR):
        lo_col = group * hidden_cols
        hi_col = lo_col + hidden_cols
        pre_part = low_back(matmul(low_back(mid_low), up_weight[:, lo_col:hi_col]) + up_bias[lo_col:hi_col])
        activ = low(smooth_gate(pre_part))
        ffn_total = ffn_total + low(matmul(activ, down_weight[:, lo_col:hi_col].T))
    ffn_out = low_back(ffn_total)
    final = norm_rows(mid + ffn_out + down_bias, norm2_gain, norm2_shift)
    row_live = (jnp.arange(SEQ_LEN, dtype=jnp.int32) < slot_len).astype(jnp.float32)[:, None]
    return final * row_live

def reference(tokens, cotangent, lengths, query_weight, key_weight, value_weight, out_weight, up_weight, down_weight, query_bias, value_bias, out_bias, norm1_gain, norm1_shift, up_bias, down_bias, norm2_gain, norm2_shift):
    params = tuple((value.astype(jnp.float32) for value in (query_weight, key_weight, value_weight, out_weight, up_weight, down_weight, query_bias, value_bias, out_bias, norm1_gain, norm1_shift, up_bias, down_bias, norm2_gain, norm2_shift)))
    inputs = tokens.astype(jnp.float32).reshape(N_DP, SEQ_LEN, D)
    cotangents = cotangent.astype(jnp.float32).reshape(N_DP, SEQ_LEN, D)

    def per_slot(totals, item):
        slot_tokens, slot_cot, slot_len = item
        outputs, back = jax.vjp(lambda value, weights: layer(value, weights, slot_len), slot_tokens, params)
        grad_value, grad_weights = back(slot_cot)
        totals = jax.tree.map(jnp.add, totals, grad_weights)
        return (totals, (outputs.astype(jnp.bfloat16), grad_value.astype(jnp.bfloat16)))
    start = jax.tree.map(jnp.zeros_like, params)
    grads, (outputs, grad_inputs) = lax.scan(per_slot, start, (inputs, cotangents, lengths))
    return (outputs.reshape(TOKENS, D), grad_inputs.reshape(TOKENS, D), grads[0], grads[1], grads[2], grads[3], grads[4], grads[5], grads[6], grads[7], grads[8], grads[9], grads[10], grads[11], grads[12], grads[13], grads[14])
```

```python
import jax
import jax.numpy as jnp
from jax import lax
from jax.experimental import pallas as pl
from jax.experimental.pallas import tpu as pltpu
from jax.sharding import PartitionSpec as P

HEADS = 16
HEAD_DIM = 128
FF = 8192
CHUNKS = 2

norm_eps = 1e-06
masked_score = -1e30
log2_e = 1.4426950408889634
score_scale = HEAD_DIM ** (-0.5)


def nt(left, right):
    return lax.dot_general(
        left, right, (((1,), (1,)), ((), ())), preferred_element_type=jnp.float32
    )


def nn(left, right):
    return lax.dot_general(
        left, right, (((1,), (0,)), ((), ())), preferred_element_type=jnp.float32
    )


def tn(left, right):
    return lax.dot_general(
        left, right, (((0,), (0,)), ((), ())), preferred_element_type=jnp.float32
    )


def low(value):
    return value.astype(jnp.bfloat16)


def wide(value):
    return value.astype(jnp.float32)


def swap(value, bits):
    size = lax.axis_size("tensor")
    return lax.ppermute(value, "tensor", [(i, i ^ bits) for i in range(size)])


def gather_rows(own):
    size = lax.axis_size("tensor")
    if size != 4:
        return jnp.concatenate([own] + [swap(own, p) for p in range(1, size)], axis=0)
    half = own.shape[0] // 2
    first, second = swap(own, 1), swap(own, 2)
    return jnp.concatenate(
        [own, first, second, swap(first[:half], 2), swap(second[half:], 1)], axis=0
    )


def scatter_sum(terms):
    size = lax.axis_size("tensor")
    rows = terms.shape[0] // size
    block = [terms[p * rows : (p + 1) * rows] for p in range(size)]
    if size != 4:
        total = wide(block[0])
        for p in range(1, size):
            total = total + wide(swap(block[p], p))
        return total
    half = rows // 2
    upper = [b[:half] for b in block]
    lower = [b[half:] for b in block]
    relay_upper = swap(upper[3], 1)
    relay_lower = swap(lower[3], 2)
    direct_upper = swap(upper[1], 1)
    direct_lower = swap(lower[2], 2)
    sum_upper = swap(low(wide(relay_upper) + wide(upper[2])), 2)
    sum_lower = swap(low(wide(relay_lower) + wide(lower[1])), 1)
    return jnp.concatenate(
        [
            wide(upper[0]) + wide(direct_upper) + wide(sum_upper),
            wide(lower[0]) + wide(direct_lower) + wide(sum_lower),
        ],
        axis=0,
    )


def all_live(limits, run, count):
    full = limits[0] >= run
    for b in range(1, count):
        full = jnp.logical_and(full, limits[b] >= run)
    return full


def mask_dead(limits, run, count, ref, filler):
    for b in range(count):

        @pl.when(limits[b] < run)
        def _():
            rows = pl.ds(b * run, run)
            row = lax.broadcasted_iota(jnp.int32, (run, ref.shape[1]), 0)
            ref[rows, :] = jnp.where(row < limits[b], ref[rows, :], filler)


def attend(chunk, projected, limits, run):
    part = projected[0].shape[0]
    chunks = len(projected)
    cols = projected[0].shape[1] // 3
    heads = cols // HEAD_DIM
    keys_n = part * chunks
    count = keys_n // run
    block = min(1024, part)
    factor = score_scale * log2_e

    def kernel(lim, q_ref, *rest):
        k_refs, v_refs = rest[:chunks], rest[chunks : 2 * chunks]
        out_ref, lse_ref, s_ref = rest[2 * chunks :]
        q = q_ref[...]
        for c in range(chunks):
            s_ref[pl.ds(c * part, part), :] = nt(k_refs[c][...], q)

        @pl.when(jnp.logical_not(all_live(lim, run, count)))
        def _():
            mask_dead(lim, run, count, s_ref, masked_score)

        s = s_ref[...]
        top = jnp.max(s, axis=0, keepdims=True) * factor
        p = jnp.exp2(s * factor - top)
        total = jnp.sum(p, axis=0, keepdims=True)
        p = low(p)
        out = tn(v_refs[0][...], p[:part])
        for c in range(1, chunks):
            out = out + tn(v_refs[c][...], p[c * part : (c + 1) * part])
        out_ref[...] = low(jnp.transpose(out / total))
        lse_ref[0] = top + jnp.log2(total)

    key_spec = pl.BlockSpec((part, HEAD_DIM), lambda h, i, lim: (0, heads + h))
    value_spec = pl.BlockSpec((part, HEAD_DIM), lambda h, i, lim: (0, 2 * heads + h))
    row_spec = pl.BlockSpec((block, HEAD_DIM), lambda h, i, lim: (i, h))
    return pl.pallas_call(
        kernel,
        out_shape=(
            jax.ShapeDtypeStruct((part, cols), jnp.bfloat16),
            jax.ShapeDtypeStruct((heads, 1, part), jnp.float32),
        ),
        grid_spec=pltpu.PrefetchScalarGridSpec(
            num_scalar_prefetch=1,
            grid=(heads, part // block),
            in_specs=[row_spec] + [key_spec] * chunks + [value_spec] * chunks,
            out_specs=[row_spec, pl.BlockSpec((1, 1, block), lambda h, i, lim: (h, 0, i))],
            scratch_shapes=[pltpu.VMEM((keys_n, block), jnp.float32)],
        ),
        compiler_params=pltpu.CompilerParams(
            dimension_semantics=("arbitrary", "arbitrary"), vmem_limit_bytes=56 * 2**20
        ),
        cost_estimate=pl.CostEstimate(
            flops=8 * keys_n * part * cols,
            transcendentals=keys_n * part * heads,
            bytes_accessed=keys_n * cols * 4 + part * cols * 4,
        ),
        name="attend",
    )(limits, projected[chunk], *projected, *projected)


def attend_back(chunk, projected, context, grad, lse, limits, run, carry):
    part = projected[0].shape[0]
    chunks = len(projected)
    cols = projected[0].shape[1] // 3
    heads = cols // HEAD_DIM
    keys_n = part * chunks
    count = keys_n // run
    block = min(1024, part)
    steps = part // block
    factor = score_scale * log2_e
    last = chunk == chunks - 1

    def kernel(lim, q_ref, o_ref, do_ref, lse_ref, *rest):
        k_refs, v_refs = rest[:chunks], rest[chunks : 2 * chunks]
        rest = rest[2 * chunks :]
        if carry is not None:
            key_in, value_in = rest[:2]
            rest = rest[2:]
        dq_ref, dk_ref, dv_ref, p_ref, key_acc, value_acc = rest
        step = pl.program_id(1)

        @pl.when(step == 0)
        def _():
            if carry is None:
                key_acc[...] = jnp.zeros_like(key_acc)
                value_acc[...] = jnp.zeros_like(value_acc)
            else:
                key_acc[...] = key_in[...]
                value_acc[...] = value_in[...]

        q = q_ref[...]
        do = do_ref[...]
        lse = lse_ref[0]
        for c in range(chunks):
            p_ref[pl.ds(c * part, part), :] = jnp.exp2(nt(k_refs[c][...], q) * factor - lse)

        @pl.when(jnp.logical_not(all_live(lim, run, count)))
        def _():
            mask_dead(lim, run, count, p_ref, 0.0)

        inner = jnp.sum(jnp.transpose(wide(do) * wide(o_ref[...])), axis=0, keepdims=True)
        dq = None
        for c in range(chunks):
            rows = pl.ds(c * part, part)
            p = p_ref[rows, :]
            ds = low(p * (nt(v_refs[c][...], do) - inner))
            value_acc[rows, :] += nn(low(p), do)
            key_acc[rows, :] += nn(ds, q)
            term = tn(k_refs[c][...], ds)
            dq = term if dq is None else dq + term
        dq_ref[...] = low(jnp.transpose(dq * score_scale))

        @pl.when(step == steps - 1)
        def _():
            if last:
                dk_ref[...] = low(key_acc[...] * score_scale)
                dv_ref[...] = low(value_acc[...])
            else:
                dk_ref[...] = key_acc[...]
                dv_ref[...] = value_acc[...]

    key_spec = pl.BlockSpec((part, HEAD_DIM), lambda h, i, lim: (0, heads + h))
    value_spec = pl.BlockSpec((part, HEAD_DIM), lambda h, i, lim: (0, 2 * heads + h))
    row_spec = pl.BlockSpec((block, HEAD_DIM), lambda h, i, lim: (i, h))
    acc_spec = pl.BlockSpec((keys_n, HEAD_DIM), lambda h, i, lim: (0, h))
    acc_type = jnp.bfloat16 if last else jnp.float32
    acc_shape = jax.ShapeDtypeStruct((keys_n, cols), acc_type)
    return pl.pallas_call(
        kernel,
        out_shape=(jax.ShapeDtypeStruct((part, cols), jnp.bfloat16), acc_shape, acc_shape),
        grid_spec=pltpu.PrefetchScalarGridSpec(
            num_scalar_prefetch=1,
            grid=(heads, steps),
            in_specs=[
                row_spec,
                row_spec,
                row_spec,
                pl.BlockSpec((1, 1, block), lambda h, i, lim: (h, 0, i)),
            ]
            + [key_spec] * chunks
            + [value_spec] * chunks
            + ([] if carry is None else [acc_spec] * 2),
            out_specs=[row_spec, acc_spec, acc_spec],
            scratch_shapes=[
                pltpu.VMEM((keys_n, block), jnp.float32),
                pltpu.VMEM((keys_n, HEAD_DIM), jnp.float32),
                pltpu.VMEM((keys_n, HEAD_DIM), jnp.float32),
            ],
        ),
        compiler_params=pltpu.CompilerParams(
            dimension_semantics=("arbitrary", "arbitrary"), vmem_limit_bytes=56 * 2**20
        ),
        cost_estimate=pl.CostEstimate(
            flops=20 * keys_n * part * cols,
            transcendentals=keys_n * part * heads,
            bytes_accessed=keys_n * cols * 16 + part * cols * 8,
        ),
        name="attend_back",
    )(
        limits,
        projected[chunk],
        context,
        grad,
        lse,
        *projected,
        *projected,
        *(() if carry is None else carry),
    )


def norm_rows(value, gain, shift):
    centred = value - jnp.mean(value, axis=-1, keepdims=True)
    inverse = lax.rsqrt(jnp.mean(centred * centred, axis=-1, keepdims=True) + norm_eps)
    unit = centred * inverse
    return (unit * gain + shift, unit, inverse)


def norm_back(grad_out, unit, inverse, gain):
    grad_unit = grad_out * gain
    inner = jnp.mean(grad_unit * unit, axis=-1, keepdims=True)
    grad_in = inverse * (grad_unit - jnp.mean(grad_unit, axis=-1, keepdims=True) - unit * inner)
    return (grad_in, jnp.sum(grad_out * unit, axis=0), jnp.sum(grad_out, axis=0))


def gate_and_slope(pre):
    ratio = (2.0 / jnp.pi) ** 0.5
    square = pre * pre
    bent = jnp.tanh(ratio * (pre + 0.044715 * square * pre))
    half = 0.5 * (1.0 + bent)
    slope = half + 0.5 * pre * (1.0 - bent * bent) * (ratio * (1.0 + 3 * 0.044715 * square))
    return low(pre * half), low(slope)


def placed(part, start, total):
    return lax.dynamic_update_slice_in_dim(jnp.zeros((total,), jnp.float32), part, start, 0)


def total_of(vectors):
    devices = lax.axis_size("dp") * lax.axis_size("tensor")
    packed = jnp.concatenate([v.reshape(devices, -1) for v in vectors], axis=1)
    packed = lax.psum_scatter(packed, ("dp", "tensor"), scatter_dimension=0, tiled=True)[0]
    sizes = [v.shape[0] // devices for v in vectors]
    parts, at = [], 0
    for size in sizes:
        parts.append(packed[at : at + size])
        at += size
    return parts


def gather_weight(weight):
    return lax.all_gather(weight, "dp", axis=0, tiled=True)


def scatter_weight(grad):
    return wide(lax.psum_scatter(low(grad), "dp", scatter_dimension=0, tiled=True))


def add_up(terms):
    total = terms[0]
    for term in terms[1:]:
        total = total + term
    return total


def per_device(
    tokens,
    cotangent,
    lengths,
    query_weight,
    key_weight,
    value_weight,
    out_weight,
    up_weight,
    down_weight,
    query_bias,
    value_bias,
    out_bias,
    norm1_gain,
    norm1_shift,
    up_bias,
    down_bias,
    norm2_gain,
    norm2_shift,
):
    rows, width = tokens.shape
    groups = lax.axis_size("tensor")
    position = lax.axis_index("tensor")
    head_cols = width // groups
    hidden_cols = FF // groups
    slot_len = lengths[0]
    col_start = position * head_cols
    hid_start = position * hidden_cols
    part = rows // CHUNKS
    cut = [slice(c * part, (c + 1) * part) for c in range(CHUNKS)]
    every = range(CHUNKS)
    limits = jnp.stack(
        [
            slot_len - ((position ^ p) * rows + c * part)
            for c in range(CHUNKS)
            for p in range(groups)
        ]
    ).astype(jnp.int32)
    row_live = (position * rows + jnp.arange(rows, dtype=jnp.int32) < slot_len).astype(jnp.float32)[
        :, None
    ]
    bias_query = lax.dynamic_slice_in_dim(query_bias, col_start, head_cols)
    bias_value = lax.dynamic_slice_in_dim(value_bias, col_start, head_cols)
    bias_up = lax.dynamic_slice_in_dim(up_bias, hid_start, hidden_cols)
    bias_proj = jnp.concatenate([bias_query, jnp.zeros_like(bias_query), bias_value])

    proj_full = gather_weight(jnp.concatenate([query_weight, key_weight, value_weight], axis=1))
    out_full = gather_weight(out_weight)
    up_full = gather_weight(up_weight)
    down_full = gather_weight(down_weight)

    seq_tokens = [gather_rows(tokens[cut[c]]) for c in every]
    projected = [low(nn(seq_tokens[c], proj_full) + bias_proj) for c in every]
    context, lse, mid, unit1, inverse1, mid_low = ([None] * CHUNKS for _ in range(6))
    for c in every:
        context[c], lse[c] = attend(c, projected, limits, part)
    for c in every:
        attn_sum = scatter_sum(low(nt(context[c], out_full)))
        mid[c], unit1[c], inverse1[c] = norm_rows(
            wide(tokens[cut[c]]) + attn_sum + out_bias, norm1_gain, norm1_shift
        )
    mid_seq = [gather_rows(low(mid[c])) for c in every]
    activ, slope = ([None] * CHUNKS for _ in range(2))
    ffn_sum = [None] * CHUNKS
    for c in every:
        activ[c], slope[c] = gate_and_slope(nn(mid_seq[c], up_full) + bias_up)
        ffn_sum[c] = scatter_sum(low(nt(activ[c], down_full)))
    layer_out, grad_sum2, vec2 = ([None] * CHUNKS for _ in range(3))
    for c in every:
        final, unit2, inverse2 = norm_rows(mid[c] + ffn_sum[c] + down_bias, norm2_gain, norm2_shift)
        layer_out[c] = low(final * row_live[cut[c]])
        grad_final = wide(cotangent[cut[c]]) * row_live[cut[c]]
        grad_sum2[c], gain_part, shift_part = norm_back(grad_final, unit2, inverse2, norm2_gain)
        vec2[c] = (gain_part, shift_part, jnp.sum(grad_sum2[c], axis=0))
    grad_ffn = [gather_rows(low(grad_sum2[c])) for c in every]
    grad_pre = [low(nn(grad_ffn[c], down_full) * wide(slope[c])) for c in every]
    mid_sum = [scatter_sum(low(nt(grad_pre[c], up_full))) for c in every]
    grad_sum1, vec1 = ([None] * CHUNKS for _ in range(2))
    for c in every:
        grad_sum1[c], gain_part, shift_part = norm_back(
            grad_sum2[c] + mid_sum[c], unit1[c], inverse1[c], norm1_gain
        )
        vec1[c] = (gain_part, shift_part, jnp.sum(grad_sum1[c], axis=0))
    grad_attn = [gather_rows(low(grad_sum1[c])) for c in every]

    down_part = scatter_weight(add_up([tn(grad_ffn[c], activ[c]) for c in every]))
    up_part = scatter_weight(add_up([tn(mid_seq[c], grad_pre[c]) for c in every]))
    out_part = scatter_weight(add_up([tn(grad_attn[c], context[c]) for c in every]))
    up_bias_part = add_up([jnp.sum(wide(grad_pre[c]), axis=0) for c in every])

    grad_query, carry = [None] * CHUNKS, None
    for c in every:
        grad_context = low(nn(grad_attn[c], out_full))
        grad_query[c], *carry = attend_back(
            c, projected, context[c], grad_context, lse[c], limits, part, carry
        )
    size = part * groups
    grad_proj = [
        jnp.concatenate([grad_query[c]] + [a[c * size : (c + 1) * size] for a in carry], axis=1)
        for c in every
    ]
    proj_part = scatter_weight(add_up([tn(seq_tokens[c], grad_proj[c]) for c in every]))
    tokens_grad = [
        low(grad_sum1[c] + scatter_sum(low(nt(grad_proj[c], proj_full)))) for c in every
    ]
    proj_bias = add_up([jnp.sum(wide(grad_proj[c]), axis=0) for c in every])
    (
        norm2_gain_grad,
        norm2_shift_grad,
        down_bias_grad,
        norm1_gain_grad,
        norm1_shift_grad,
        out_bias_grad,
        up_bias_grad,
    ) = total_of(
        [add_up([vec2[c][i] for c in every]) for i in range(3)]
        + [add_up([vec1[c][i] for c in every]) for i in range(3)]
        + [placed(up_bias_part, hid_start, FF)]
    )
    query_bias_grad, value_bias_grad = total_of(
        [
            placed(proj_bias[:head_cols], col_start, width),
            placed(proj_bias[2 * head_cols :], col_start, width),
        ]
    )
    return (
        jnp.concatenate(layer_out, axis=0),
        jnp.concatenate(tokens_grad, axis=0),
        proj_part[:, :head_cols],
        proj_part[:, head_cols : 2 * head_cols],
        proj_part[:, 2 * head_cols :],
        out_part,
        up_part,
        down_part,
        query_bias_grad,
        value_bias_grad,
        out_bias_grad,
        norm1_gain_grad,
        norm1_shift_grad,
        up_bias_grad,
        down_bias_grad,
        norm2_gain_grad,
        norm2_shift_grad,
    )


def solution(mesh):
    row = P(("dp", "tensor"), None)
    block = P("dp", "tensor")
    share = P(("dp", "tensor"))
    return jax.shard_map(
        per_device,
        mesh=mesh,
        in_specs=(row, row, P("dp")) + (block,) * 6 + (P(),) * 9,
        out_specs=(row, row) + (block,) * 6 + (share,) * 9,
        check_vma=False,
    )
```

```python
import jax
import jax.numpy as jnp
from jax import lax
from jax.experimental import pallas as pl
from jax.experimental.pallas import tpu as pltpu
from jax.sharding import PartitionSpec as P

HEADS = 16
HEAD_DIM = 128
FF = 8192
CHUNKS = 2

norm_eps = 1e-06
masked_score = -1e30
log2_e = 1.4426950408889634
score_scale = HEAD_DIM ** (-0.5)


def nt(left, right):
    return lax.dot_general(
        left, right, (((1,), (1,)), ((), ())), preferred_element_type=jnp.float32
    )


def nn(left, right):
    return lax.dot_general(
        left, right, (((1,), (0,)), ((), ())), preferred_element_type=jnp.float32
    )


def tn(left, right):
    return lax.dot_general(
        left, right, (((0,), (0,)), ((), ())), preferred_element_type=jnp.float32
    )


def low(value):
    return value.astype(jnp.bfloat16)


def wide(value):
    return value.astype(jnp.float32)


def swap(value, bits):
    size = lax.axis_size("tensor")
    return lax.ppermute(value, "tensor", [(i, i ^ bits) for i in range(size)])


def after(value, *others):
    return lax.optimization_barrier((value, *others))[0]


def gather_near(own):
    size = lax.axis_size("tensor")
    if size != 4:
        return [own] + [swap(own, p) for p in range(1, size)]
    return [own, swap(own, 1), swap(own, 2)]


def gather_far(near, *others):
    if lax.axis_size("tensor") != 4:
        return jnp.concatenate(near, axis=0)
    half = near[0].shape[0] // 2
    upper, lower = after(near[1][:half], *others), after(near[2][half:], *others)
    return jnp.concatenate(near + [swap(upper, 2), swap(lower, 1)], axis=0)


def scatter_near(terms):
    size = lax.axis_size("tensor")
    rows = terms.shape[0] // size
    block = [terms[p * rows : (p + 1) * rows] for p in range(size)]
    if size != 4:
        return block, [swap(block[p], p) for p in range(1, size)]
    half = rows // 2
    return block, [
        swap(block[3][:half], 1),
        swap(block[3][half:], 2),
        swap(block[1][:half], 1),
        swap(block[2][half:], 2),
    ]


def scatter_far(near, *others):
    block, came = near
    if lax.axis_size("tensor") != 4:
        return add_up([wide(block[0])] + [wide(c) for c in came])
    half = block[0].shape[0] // 2
    upper = low(wide(came[0]) + wide(block[2][:half]))
    lower = low(wide(came[1]) + wide(block[1][half:]))
    sum_upper = swap(after(upper, *others), 2)
    sum_lower = swap(after(lower, *others), 1)
    return jnp.concatenate(
        [
            wide(block[0][:half]) + wide(came[2]) + wide(sum_upper),
            wide(block[0][half:]) + wide(came[3]) + wide(sum_lower),
        ],
        axis=0,
    )


def all_live(limits, run, count):
    full = limits[0] >= run
    for b in range(1, count):
        full = jnp.logical_and(full, limits[b] >= run)
    return full


def mask_dead(limits, run, count, ref, filler):
    for b in range(count):

        @pl.when(limits[b] < run)
        def _():
            rows = pl.ds(b * run, run)
            row = lax.broadcasted_iota(jnp.int32, (run, ref.shape[1]), 0)
            ref[rows, :] = jnp.where(row < limits[b], ref[rows, :], filler)


def attend(chunk, projected, limits, run):
    part = projected[0].shape[0]
    chunks = len(projected)
    cols = projected[0].shape[1] // 3
    heads = cols // HEAD_DIM
    keys_n = part * chunks
    count = keys_n // run
    block = min(1024, part)
    factor = score_scale * log2_e

    def kernel(lim, q_ref, *rest):
        k_refs, v_refs = rest[:chunks], rest[chunks : 2 * chunks]
        out_ref, lse_ref, s_ref = rest[2 * chunks :]
        q = q_ref[...]
        for c in range(chunks):
            s_ref[pl.ds(c * part, part), :] = nt(k_refs[c][...], q)

        @pl.when(jnp.logical_not(all_live(lim, run, count)))
        def _():
            mask_dead(lim, run, count, s_ref, masked_score)

        s = s_ref[...]
        top = jnp.max(s, axis=0, keepdims=True) * factor
        p = jnp.exp2(s * factor - top)
        total = jnp.sum(p, axis=0, keepdims=True)
        p = low(p)
        out = tn(v_refs[0][...], p[:part])
        for c in range(1, chunks):
            out = out + tn(v_refs[c][...], p[c * part : (c + 1) * part])
        out_ref[...] = low(jnp.transpose(out / total))
        lse_ref[0] = top + jnp.log2(total)

    key_spec = pl.BlockSpec((part, HEAD_DIM), lambda h, i, lim: (0, heads + h))
    value_spec = pl.BlockSpec((part, HEAD_DIM), lambda h, i, lim: (0, 2 * heads + h))
    row_spec = pl.BlockSpec((block, HEAD_DIM), lambda h, i, lim: (i, h))
    return pl.pallas_call(
        kernel,
        out_shape=(
            jax.ShapeDtypeStruct((part, cols), jnp.bfloat16),
            jax.ShapeDtypeStruct((heads, 1, part), jnp.float32),
        ),
        grid_spec=pltpu.PrefetchScalarGridSpec(
            num_scalar_prefetch=1,
            grid=(heads, part // block),
            in_specs=[row_spec] + [key_spec] * chunks + [value_spec] * chunks,
            out_specs=[row_spec, pl.BlockSpec((1, 1, block), lambda h, i, lim: (h, 0, i))],
            scratch_shapes=[pltpu.VMEM((keys_n, block), jnp.float32)],
        ),
        compiler_params=pltpu.CompilerParams(
            dimension_semantics=("arbitrary", "arbitrary"), vmem_limit_bytes=56 * 2**20
        ),
        cost_estimate=pl.CostEstimate(
            flops=8 * keys_n * part * cols,
            transcendentals=keys_n * part * heads,
            bytes_accessed=keys_n * cols * 4 + part * cols * 4,
        ),
        name="attend",
    )(limits, projected[chunk], *projected, *projected)


def attend_back(chunk, projected, context, grad, lse, limits, run, carry):
    part = projected[0].shape[0]
    chunks = len(projected)
    cols = projected[0].shape[1] // 3
    heads = cols // HEAD_DIM
    keys_n = part * chunks
    count = keys_n // run
    block = min(1024, part)
    steps = part // block
    factor = score_scale * log2_e
    last = chunk == chunks - 1

    def kernel(lim, q_ref, o_ref, do_ref, lse_ref, *rest):
        k_refs, v_refs = rest[:chunks], rest[chunks : 2 * chunks]
        rest = rest[2 * chunks :]
        if carry is not None:
            key_in, value_in = rest[:2]
            rest = rest[2:]
        dq_ref, dk_ref, dv_ref, p_ref, key_acc, value_acc = rest
        step = pl.program_id(1)

        @pl.when(step == 0)
        def _():
            if carry is None:
                key_acc[...] = jnp.zeros_like(key_acc)
                value_acc[...] = jnp.zeros_like(value_acc)
            else:
                key_acc[...] = key_in[...]
                value_acc[...] = value_in[...]

        q = q_ref[...]
        do = do_ref[...]
        lse = lse_ref[0]
        for c in range(chunks):
            p_ref[pl.ds(c * part, part), :] = jnp.exp2(nt(k_refs[c][...], q) * factor - lse)

        @pl.when(jnp.logical_not(all_live(lim, run, count)))
        def _():
            mask_dead(lim, run, count, p_ref, 0.0)

        inner = jnp.sum(jnp.transpose(wide(do) * wide(o_ref[...])), axis=0, keepdims=True)
        dq = None
        for c in range(chunks):
            rows = pl.ds(c * part, part)
            p = p_ref[rows, :]
            ds = low(p * (nt(v_refs[c][...], do) - inner))
            value_acc[rows, :] += nn(low(p), do)
            key_acc[rows, :] += nn(ds, q)
            term = tn(k_refs[c][...], ds)
            dq = term if dq is None else dq + term
        dq_ref[...] = low(jnp.transpose(dq * score_scale))

        @pl.when(step == steps - 1)
        def _():
            if last:
                dk_ref[...] = low(key_acc[...] * score_scale)
                dv_ref[...] = low(value_acc[...])
            else:
                dk_ref[...] = key_acc[...]
                dv_ref[...] = value_acc[...]

    key_spec = pl.BlockSpec((part, HEAD_DIM), lambda h, i, lim: (0, heads + h))
    value_spec = pl.BlockSpec((part, HEAD_DIM), lambda h, i, lim: (0, 2 * heads + h))
    row_spec = pl.BlockSpec((block, HEAD_DIM), lambda h, i, lim: (i, h))
    acc_spec = pl.BlockSpec((keys_n, HEAD_DIM), lambda h, i, lim: (0, h))
    acc_type = jnp.bfloat16 if last else jnp.float32
    acc_shape = jax.ShapeDtypeStruct((keys_n, cols), acc_type)
    return pl.pallas_call(
        kernel,
        out_shape=(jax.ShapeDtypeStruct((part, cols), jnp.bfloat16), acc_shape, acc_shape),
        grid_spec=pltpu.PrefetchScalarGridSpec(
            num_scalar_prefetch=1,
            grid=(heads, steps),
            in_specs=[
                row_spec,
                row_spec,
                row_spec,
                pl.BlockSpec((1, 1, block), lambda h, i, lim: (h, 0, i)),
            ]
            + [key_spec] * chunks
            + [value_spec] * chunks
            + ([] if carry is None else [acc_spec] * 2),
            out_specs=[row_spec, acc_spec, acc_spec],
            scratch_shapes=[
                pltpu.VMEM((keys_n, block), jnp.float32),
                pltpu.VMEM((keys_n, HEAD_DIM), jnp.float32),
                pltpu.VMEM((keys_n, HEAD_DIM), jnp.float32),
            ],
        ),
        compiler_params=pltpu.CompilerParams(
            dimension_semantics=("arbitrary", "arbitrary"), vmem_limit_bytes=56 * 2**20
        ),
        cost_estimate=pl.CostEstimate(
            flops=20 * keys_n * part * cols,
            transcendentals=keys_n * part * heads,
            bytes_accessed=keys_n * cols * 16 + part * cols * 8,
        ),
        name="attend_back",
    )(
        limits,
        projected[chunk],
        context,
        grad,
        lse,
        *projected,
        *projected,
        *(() if carry is None else carry),
    )


def norm_rows(value, gain, shift):
    centred = value - jnp.mean(value, axis=-1, keepdims=True)
    inverse = lax.rsqrt(jnp.mean(centred * centred, axis=-1, keepdims=True) + norm_eps)
    unit = centred * inverse
    return (unit * gain + shift, unit, inverse)


def norm_back(grad_out, unit, inverse, gain):
    grad_unit = grad_out * gain
    inner = jnp.mean(grad_unit * unit, axis=-1, keepdims=True)
    grad_in = inverse * (grad_unit - jnp.mean(grad_unit, axis=-1, keepdims=True) - unit * inner)
    return (grad_in, jnp.sum(grad_out * unit, axis=0), jnp.sum(grad_out, axis=0))


def gate_and_slope(pre):
    ratio = (2.0 / jnp.pi) ** 0.5
    square = pre * pre
    bent = jnp.tanh(ratio * (pre + 0.044715 * square * pre))
    half = 0.5 * (1.0 + bent)
    slope = half + 0.5 * pre * (1.0 - bent * bent) * (ratio * (1.0 + 3 * 0.044715 * square))
    return low(pre * half), low(slope)


def placed(part, start, total):
    return lax.dynamic_update_slice_in_dim(jnp.zeros((total,), jnp.float32), part, start, 0)


def total_of(vectors):
    slots, groups = lax.axis_size("dp"), lax.axis_size("tensor")
    slot, position = lax.axis_index("dp"), lax.axis_index("tensor")
    packed = jnp.concatenate([v.reshape(slots, groups, -1) for v in vectors], axis=2)

    def share(p):
        return lax.dynamic_index_in_dim(packed, position ^ p, 1, keepdims=False)

    total = add_up([share(0)] + [swap(share(p), p) for p in range(1, groups)])

    def ahead(step):
        return lax.dynamic_index_in_dim(total, (slot + step) % slots, 0, keepdims=False)

    total = add_up(
        [ahead(0)]
        + [
            lax.ppermute(ahead(step), "dp", [(i, (i + step) % slots) for i in range(slots)])
            for step in range(1, slots)
        ]
    )
    parts, at = [], 0
    for v in vectors:
        size = v.shape[0] // (slots * groups)
        parts.append(total[at : at + size])
        at += size
    return parts


def gather_weight(weight):
    return lax.all_gather(weight, "dp", axis=0, tiled=True)


def scatter_weight(grad):
    return lax.psum_scatter(grad, "dp", scatter_dimension=0, tiled=True)


def add_up(terms):
    total = terms[0]
    for term in terms[1:]:
        total = total + term
    return total


def per_device(
    tokens,
    cotangent,
    lengths,
    query_weight,
    key_weight,
    value_weight,
    out_weight,
    up_weight,
    down_weight,
    query_bias,
    value_bias,
    out_bias,
    norm1_gain,
    norm1_shift,
    up_bias,
    down_bias,
    norm2_gain,
    norm2_shift,
):
    rows, width = tokens.shape
    groups = lax.axis_size("tensor")
    position = lax.axis_index("tensor")
    head_cols = width // groups
    hidden_cols = FF // groups
    slot_len = lengths[0]
    col_start = position * head_cols
    hid_start = position * hidden_cols
    part = rows // CHUNKS
    cut = [slice(c * part, (c + 1) * part) for c in range(CHUNKS)]
    every = range(CHUNKS)
    limits = jnp.stack(
        [
            slot_len - ((position ^ p) * rows + c * part)
            for c in range(CHUNKS)
            for p in range(groups)
        ]
    ).astype(jnp.int32)
    row_live = (position * rows + jnp.arange(rows, dtype=jnp.int32) < slot_len).astype(jnp.float32)[
        :, None
    ]
    bias_query = lax.dynamic_slice_in_dim(query_bias, col_start, head_cols)
    bias_value = lax.dynamic_slice_in_dim(value_bias, col_start, head_cols)
    bias_up = lax.dynamic_slice_in_dim(up_bias, hid_start, hidden_cols)
    bias_proj = jnp.concatenate([bias_query, jnp.zeros_like(bias_query), bias_value])

    proj_full = gather_weight(jnp.concatenate([query_weight, key_weight, value_weight], axis=1))
    out_full = gather_weight(out_weight)
    up_full = gather_weight(up_weight)
    down_full = gather_weight(down_weight)

    def lists(count):
        return ([None] * CHUNKS for _ in range(count))

    near, seq_tokens, projected = lists(3)
    for c in every:
        near[c] = gather_near(after(tokens[cut[c]], *(near[c - 1] if c else ())))
    for c in every:
        seq_tokens[c] = gather_far(near[c])
        projected[c] = low(nn(seq_tokens[c], proj_full) + bias_proj)
    context, lse, attn_low = lists(3)
    for c in every:
        queries = projected if c == 0 else [after(p, attn_low[c - 1]) for p in projected]
        context[c], lse[c] = attend(c, queries, limits, part)
        attn_low[c] = low(nt(context[c], out_full))
        near[c] = scatter_near(attn_low[c])
    mid, mid_out, unit1, inverse1, mid_near = lists(5)
    before = attn_low[-1]
    for c in every:
        attn_sum = scatter_far(near[c], before)
        mid[c], unit1[c], inverse1[c] = norm_rows(
            wide(tokens[cut[c]]) + attn_sum + out_bias, norm1_gain, norm1_shift
        )
        before = mid_out[c] = low(mid[c])
    for c in every:
        mid_near[c] = gather_near(after(mid_out[c], *(mid_near[c - 1] if c else ())))
    mid_seq, activ, slope, ffn_low, ffn_near = lists(5)
    before = mid_out[-1]
    for c in every:
        mid_seq[c] = gather_far(mid_near[c], before)
        source = mid_seq[c] if c == 0 else after(mid_seq[c], ffn_low[c - 1])
        activ[c], slope[c] = gate_and_slope(nn(source, up_full) + bias_up)
        ffn_low[c] = low(nt(activ[c], down_full))
        ffn_near[c] = scatter_near(ffn_low[c])
        before = activ[c]
    layer_out, grad_sum2, grad_out2, vec2, grad_near = lists(5)
    before = ffn_low[-1]
    for c in every:
        ffn_sum = scatter_far(ffn_near[c], before)
        final, unit2, inverse2 = norm_rows(mid[c] + ffn_sum + down_bias, norm2_gain, norm2_shift)
        layer_out[c] = low(final * row_live[cut[c]])
        grad_final = wide(cotangent[cut[c]]) * row_live[cut[c]]
        grad_sum2[c], gain_part, shift_part = norm_back(grad_final, unit2, inverse2, norm2_gain)
        vec2[c] = (gain_part, shift_part, jnp.sum(grad_sum2[c], axis=0))
        before = grad_out2[c] = low(grad_sum2[c])
    for c in every:
        grad_near[c] = gather_near(after(grad_out2[c], *(grad_near[c - 1] if c else ())))
    grad_ffn, grad_pre, mid_low, mid_back = lists(4)
    before = grad_out2[-1]
    for c in every:
        grad_ffn[c] = gather_far(grad_near[c], before)
        source = grad_ffn[c] if c == 0 else after(grad_ffn[c], mid_low[c - 1])
        grad_pre[c] = low(nn(source, down_full) * wide(slope[c]))
        mid_low[c] = low(nt(grad_pre[c], up_full))
        mid_back[c] = scatter_near(mid_low[c])
        before = grad_pre[c]
    early = (mid_low[-1], *mid_back[0][1])
    down_grad = low(add_up([tn(after(grad_ffn[c], *early), activ[c]) for c in every]))
    down_part = scatter_weight(down_grad)
    up_bias_part = add_up([jnp.sum(wide(grad_pre[c]), axis=0) for c in every])

    grad_sum1, grad_out1, vec1, attn_near = lists(4)
    before = (mid_low[-1],)
    for c in every:
        mid_sum = scatter_far(mid_back[c], *before)
        grad_sum1[c], gain_part, shift_part = norm_back(
            grad_sum2[c] + mid_sum, unit1[c], inverse1[c], norm1_gain
        )
        vec1[c] = (gain_part, shift_part, jnp.sum(grad_sum1[c], axis=0))
        grad_out1[c] = low(grad_sum1[c])
        before = (grad_out1[c], down_grad)
    up_grad = low(add_up([tn(after(mid_seq[c], grad_out1[0]), grad_pre[c]) for c in every]))
    up_part = scatter_weight(up_grad)
    for c in every:
        attn_near[c] = gather_near(after(grad_out1[c], *(attn_near[c - 1] if c else ())))
    grad_attn, grad_query = lists(2)
    carry = None
    before = (grad_out1[-1],)
    for c in every:
        grad_attn[c] = gather_far(attn_near[c], *before)
        source = after(grad_attn[c], grad_query[c - 1] if c else up_grad)
        grad_context = low(nn(source, out_full))
        grad_query[c], *carry = attend_back(
            c, projected, context[c], grad_context, lse[c], limits, part, carry
        )
        before = (grad_query[c], down_part)
    out_grad = low(add_up([tn(grad_attn[c], context[c]) for c in every]))
    out_part = scatter_weight(out_grad)
    size = part * groups
    grad_proj = [
        jnp.concatenate([grad_query[c]] + [a[c * size : (c + 1) * size] for a in carry], axis=1)
        for c in every
    ]
    proj_grad = low(add_up([tn(seq_tokens[c], grad_proj[c]) for c in every]))
    proj_part = scatter_weight(proj_grad)
    tokens_low, tokens_near, tokens_grad = lists(3)
    for c in every:
        tokens_low[c] = low(nt(after(grad_proj[c], proj_grad, up_part), proj_full))
        tokens_near[c] = scatter_near(tokens_low[c])
    before = (tokens_low[-1],)
    for c in every:
        tokens_grad[c] = low(grad_sum1[c] + scatter_far(tokens_near[c], *before))
        before = (out_part,)
    proj_part, out_part, up_part, down_part = map(wide, (proj_part, out_part, up_part, down_part))
    proj_bias = add_up([jnp.sum(wide(grad_proj[c]), axis=0) for c in every])
    (
        norm2_gain_grad,
        norm2_shift_grad,
        down_bias_grad,
        norm1_gain_grad,
        norm1_shift_grad,
        out_bias_grad,
        up_bias_grad,
        query_bias_grad,
        value_bias_grad,
    ) = total_of(
        [add_up([vec2[c][i] for c in every]) for i in range(3)]
        + [add_up([vec1[c][i] for c in every]) for i in range(3)]
        + [
            placed(up_bias_part, hid_start, FF),
            placed(proj_bias[:head_cols], col_start, width),
            placed(proj_bias[2 * head_cols :], col_start, width),
        ]
    )
    return (
        jnp.concatenate(layer_out, axis=0),
        jnp.concatenate(tokens_grad, axis=0),
        proj_part[:, :head_cols],
        proj_part[:, head_cols : 2 * head_cols],
        proj_part[:, 2 * head_cols :],
        out_part,
        up_part,
        down_part,
        query_bias_grad,
        value_bias_grad,
        out_bias_grad,
        norm1_gain_grad,
        norm1_shift_grad,
        up_bias_grad,
        down_bias_grad,
        norm2_gain_grad,
        norm2_shift_grad,
    )


def solution(mesh):
    row = P(("dp", "tensor"), None)
    block = P("dp", "tensor")
    share = P(("dp", "tensor"))
    return jax.shard_map(
        per_device,
        mesh=mesh,
        in_specs=(row, row, P("dp")) + (block,) * 6 + (P(),) * 9,
        out_specs=(row, row) + (block,) * 6 + (share,) * 9,
        check_vma=False,
    )
```

```python
import jax
import jax.numpy as jnp
from jax import lax
from jax.experimental import pallas as pl
from jax.experimental.pallas import tpu as pltpu
from jax.sharding import PartitionSpec as P

HEADS = 16
HEAD_DIM = 128
FF = 8192
CHUNKS = 2

norm_eps = 1e-06
masked_score = -1e30
log2_e = 1.4426950408889634
score_scale = HEAD_DIM ** (-0.5)


def nt(left, right):
    return lax.dot_general(
        left, right, (((1,), (1,)), ((), ())), preferred_element_type=jnp.float32
    )


def nn(left, right):
    return lax.dot_general(
        left, right, (((1,), (0,)), ((), ())), preferred_element_type=jnp.float32
    )


def tn(left, right):
    return lax.dot_general(
        left, right, (((0,), (0,)), ((), ())), preferred_element_type=jnp.float32
    )


def low(value):
    return value.astype(jnp.bfloat16)


def wide(value):
    return value.astype(jnp.float32)


def half_order():
    size = lax.axis_size("tensor")
    if size != 4:
        return [(p, side) for p in range(size) for side in range(2)]
    return [(0, 0), (0, 1), (1, 1), (2, 0), (3, 0), (1, 0), (3, 1), (2, 1)]


def swap(value, bits):
    size = lax.axis_size("tensor")
    return lax.ppermute(value, "tensor", [(i, i ^ bits) for i in range(size)])


def after(value, *others):
    return lax.optimization_barrier((value, *others))[0]


def together(values, *others):
    values = tuple(values)
    return lax.optimization_barrier((*values, *others))[: len(values)]


def gather_near(own, *others):
    size = lax.axis_size("tensor")
    own = after(own, *others)
    return [swap(own, p) for p in range(1, 3 if size == 4 else size)]


def gather_far(near, *others):
    if lax.axis_size("tensor") != 4:
        return []
    half = near[0].shape[0] // 2
    near = together(near, *others)
    return [swap(near[0][:half], 2), swap(near[1][half:], 1)]


def gathered(own, near, far):
    if not far:
        return jnp.concatenate([own] + near, axis=0)
    half = own.shape[0] // 2
    first, second = near
    return jnp.concatenate(
        [own, first[half:], second[:half], far[0], first[:half], far[1], second[half:]], axis=0
    )


def scatter_near(terms, *others):
    size = lax.axis_size("tensor")
    rows = terms.shape[0] // size
    terms = after(terms, *others)
    if size != 4:
        return terms[:rows], [swap(terms[p * rows : (p + 1) * rows], p) for p in range(1, size)]
    return terms[: 2 * rows], [
        swap(terms[2 * rows : 3 * rows], 1),
        swap(terms[3 * rows :], 2),
    ]


def scatter_sums(near, *others):
    if lax.axis_size("tensor") != 4:
        return []
    kept, came = near
    first, second = together(came, *others)
    half = kept.shape[0] // 4
    lower = low(wide(second[:half]) + wide(kept[2 * half : 3 * half]))
    upper = low(wide(first[:half]) + wide(kept[3 * half :]))
    return together((lower, upper))


def scatter_far(near, *others):
    return [swap(value, p) for p, value in enumerate(scatter_sums(near, *others), 1)]


def scatter_far_gather_near(near, own, *others):
    sums = scatter_sums(near, *others)
    if not sums:
        return [], gather_near(own, *near[1], *others)
    half = sums[0].shape[0]
    pieces = together([jnp.concatenate([value, own], axis=0) for value in sums])
    came = [swap(value, p) for p, value in enumerate(pieces, 1)]
    return [c[:half] for c in came], [c[half:] for c in came]


def scattered(near, far):
    kept, came = near
    if not far:
        return add_up([wide(kept)] + [wide(c) for c in came])
    half = kept.shape[0] // 4
    return jnp.concatenate(
        [
            wide(kept[:half]) + wide(came[0][half:]) + wide(far[1]),
            wide(kept[half : 2 * half]) + wide(came[1][half:]) + wide(far[0]),
        ],
        axis=0,
    )


def all_live(limits, run, count):
    full = limits[0] >= run
    for b in range(1, count):
        full = jnp.logical_and(full, limits[b] >= run)
    return full


def mask_dead(limits, run, count, ref, filler):
    for b in range(count):

        @pl.when(limits[b] < run)
        def _():
            rows = pl.ds(b * run, run)
            row = lax.broadcasted_iota(jnp.int32, (run, ref.shape[1]), 0)
            ref[rows, :] = jnp.where(row < limits[b], ref[rows, :], filler)


def attend(chunk, projected, limits, run):
    part = projected[0].shape[0]
    chunks = len(projected)
    cols = projected[0].shape[1] // 3
    heads = cols // HEAD_DIM
    keys_n = part * chunks
    count = keys_n // run
    block = min(1024, part)
    factor = score_scale * log2_e

    def kernel(lim, q_ref, *rest):
        k_refs, v_refs = rest[:chunks], rest[chunks : 2 * chunks]
        out_ref, lse_ref, s_ref = rest[2 * chunks :]
        q = q_ref[...]
        for c in range(chunks):
            s_ref[pl.ds(c * part, part), :] = nt(k_refs[c][...], q)

        @pl.when(jnp.logical_not(all_live(lim, run, count)))
        def _():
            mask_dead(lim, run, count, s_ref, masked_score)

        s = s_ref[...]
        top = jnp.max(s, axis=0, keepdims=True) * factor
        p = jnp.exp2(s * factor - top)
        total = jnp.sum(p, axis=0, keepdims=True)
        p = low(p)
        out = tn(v_refs[0][...], p[:part])
        for c in range(1, chunks):
            out = out + tn(v_refs[c][...], p[c * part : (c + 1) * part])
        out_ref[...] = low(jnp.transpose(out / total))
        lse_ref[0] = top + jnp.log2(total)

    key_spec = pl.BlockSpec((part, HEAD_DIM), lambda h, i, lim: (0, heads + h))
    value_spec = pl.BlockSpec((part, HEAD_DIM), lambda h, i, lim: (0, 2 * heads + h))
    row_spec = pl.BlockSpec((block, HEAD_DIM), lambda h, i, lim: (i, h))
    return pl.pallas_call(
        kernel,
        out_shape=(
            jax.ShapeDtypeStruct((part, cols), jnp.bfloat16),
            jax.ShapeDtypeStruct((heads, 1, part), jnp.float32),
        ),
        grid_spec=pltpu.PrefetchScalarGridSpec(
            num_scalar_prefetch=1,
            grid=(heads, part // block),
            in_specs=[row_spec] + [key_spec] * chunks + [value_spec] * chunks,
            out_specs=[row_spec, pl.BlockSpec((1, 1, block), lambda h, i, lim: (h, 0, i))],
            scratch_shapes=[pltpu.VMEM((keys_n, block), jnp.float32)],
        ),
        compiler_params=pltpu.CompilerParams(
            dimension_semantics=("arbitrary", "arbitrary"), vmem_limit_bytes=56 * 2**20
        ),
        cost_estimate=pl.CostEstimate(
            flops=8 * keys_n * part * cols,
            transcendentals=keys_n * part * heads,
            bytes_accessed=keys_n * cols * 4 + part * cols * 4,
        ),
        name="attend",
    )(limits, projected[chunk], *projected, *projected)


def attend_back(chunk, projected, context, grad, lse, limits, run, carry):
    part = projected[0].shape[0]
    chunks = len(projected)
    cols = projected[0].shape[1] // 3
    heads = cols // HEAD_DIM
    keys_n = part * chunks
    count = keys_n // run
    block = min(1024, part)
    steps = part // block
    factor = score_scale * log2_e
    last = chunk == chunks - 1

    def kernel(lim, q_ref, o_ref, do_ref, lse_ref, *rest):
        k_refs, v_refs = rest[:chunks], rest[chunks : 2 * chunks]
        rest = rest[2 * chunks :]
        if carry is not None:
            key_in, value_in = rest[:2]
            rest = rest[2:]
        dq_ref, dk_ref, dv_ref, p_ref, key_acc, value_acc = rest
        step = pl.program_id(1)

        @pl.when(step == 0)
        def _():
            if carry is None:
                key_acc[...] = jnp.zeros_like(key_acc)
                value_acc[...] = jnp.zeros_like(value_acc)
            else:
                key_acc[...] = key_in[...]
                value_acc[...] = value_in[...]

        q = q_ref[...]
        do = do_ref[...]
        lse = lse_ref[0]
        for c in range(chunks):
            p_ref[pl.ds(c * part, part), :] = jnp.exp2(nt(k_refs[c][...], q) * factor - lse)

        @pl.when(jnp.logical_not(all_live(lim, run, count)))
        def _():
            mask_dead(lim, run, count, p_ref, 0.0)

        inner = jnp.sum(jnp.transpose(wide(do) * wide(o_ref[...])), axis=0, keepdims=True)
        dq = None
        for c in range(chunks):
            rows = pl.ds(c * part, part)
            p = p_ref[rows, :]
            ds = low(p * (nt(v_refs[c][...], do) - inner))
            value_acc[rows, :] += nn(low(p), do)
            key_acc[rows, :] += nn(ds, q)
            term = tn(k_refs[c][...], ds)
            dq = term if dq is None else dq + term
        dq_ref[...] = low(jnp.transpose(dq * score_scale))

        @pl.when(step == steps - 1)
        def _():
            if last:
                dk_ref[...] = low(key_acc[...] * score_scale)
                dv_ref[...] = low(value_acc[...])
            else:
                dk_ref[...] = key_acc[...]
                dv_ref[...] = value_acc[...]

    key_spec = pl.BlockSpec((part, HEAD_DIM), lambda h, i, lim: (0, heads + h))
    value_spec = pl.BlockSpec((part, HEAD_DIM), lambda h, i, lim: (0, 2 * heads + h))
    row_spec = pl.BlockSpec((block, HEAD_DIM), lambda h, i, lim: (i, h))
    acc_spec = pl.BlockSpec((keys_n, HEAD_DIM), lambda h, i, lim: (0, h))
    acc_type = jnp.bfloat16 if last else jnp.float32
    acc_shape = jax.ShapeDtypeStruct((keys_n, cols), acc_type)
    return pl.pallas_call(
        kernel,
        out_shape=(jax.ShapeDtypeStruct((part, cols), jnp.bfloat16), acc_shape, acc_shape),
        grid_spec=pltpu.PrefetchScalarGridSpec(
            num_scalar_prefetch=1,
            grid=(heads, steps),
            in_specs=[
                row_spec,
                row_spec,
                row_spec,
                pl.BlockSpec((1, 1, block), lambda h, i, lim: (h, 0, i)),
            ]
            + [key_spec] * chunks
            + [value_spec] * chunks
            + ([] if carry is None else [acc_spec] * 2),
            out_specs=[row_spec, acc_spec, acc_spec],
            scratch_shapes=[
                pltpu.VMEM((keys_n, block), jnp.float32),
                pltpu.VMEM((keys_n, HEAD_DIM), jnp.float32),
                pltpu.VMEM((keys_n, HEAD_DIM), jnp.float32),
            ],
        ),
        compiler_params=pltpu.CompilerParams(
            dimension_semantics=("arbitrary", "arbitrary"), vmem_limit_bytes=56 * 2**20
        ),
        cost_estimate=pl.CostEstimate(
            flops=20 * keys_n * part * cols,
            transcendentals=keys_n * part * heads,
            bytes_accessed=keys_n * cols * 16 + part * cols * 8,
        ),
        name="attend_back",
    )(
        limits,
        projected[chunk],
        context,
        grad,
        lse,
        *projected,
        *projected,
        *(() if carry is None else carry),
    )


def norm_rows(value, gain, shift):
    centred = value - jnp.mean(value, axis=-1, keepdims=True)
    inverse = lax.rsqrt(jnp.mean(centred * centred, axis=-1, keepdims=True) + norm_eps)
    unit = centred * inverse
    return (unit * gain + shift, unit, inverse)


def norm_back(grad_out, unit, inverse, gain):
    grad_unit = grad_out * gain
    inner = jnp.mean(grad_unit * unit, axis=-1, keepdims=True)
    grad_in = inverse * (grad_unit - jnp.mean(grad_unit, axis=-1, keepdims=True) - unit * inner)
    return (grad_in, jnp.sum(grad_out * unit, axis=0), jnp.sum(grad_out, axis=0))


def gate_and_slope(pre):
    ratio = (2.0 / jnp.pi) ** 0.5
    square = pre * pre
    bent = jnp.tanh(ratio * (pre + 0.044715 * square * pre))
    half = 0.5 * (1.0 + bent)
    slope = half + 0.5 * pre * (1.0 - bent * bent) * (ratio * (1.0 + 3 * 0.044715 * square))
    return low(pre * half), low(slope)


def placed(part, start, total):
    return lax.dynamic_update_slice_in_dim(jnp.zeros((total,), jnp.float32), part, start, 0)


def total_of(vectors):
    slots, groups = lax.axis_size("dp"), lax.axis_size("tensor")
    slot, position = lax.axis_index("dp"), lax.axis_index("tensor")
    packed = jnp.concatenate([v.reshape(slots, groups, -1) for v in vectors], axis=2)

    def share(p):
        return lax.dynamic_index_in_dim(packed, position ^ p, 1, keepdims=False)

    total = add_up([share(0)] + [swap(share(p), p) for p in range(1, groups)])

    def ahead(step):
        return lax.dynamic_index_in_dim(total, (slot + step) % slots, 0, keepdims=False)

    total = add_up(
        [ahead(0)]
        + [
            lax.ppermute(ahead(step), "dp", [(i, (i + step) % slots) for i in range(slots)])
            for step in range(1, slots)
        ]
    )
    parts, at = [], 0
    for v in vectors:
        size = v.shape[0] // (slots * groups)
        parts.append(total[at : at + size])
        at += size
    return parts


def gather_weight(weight):
    return lax.all_gather(weight, "dp", axis=0, tiled=True)


def scatter_weight(grad):
    return lax.psum_scatter(grad, "dp", scatter_dimension=0, tiled=True)


def pair_exchange(grad):
    slots = lax.axis_size("dp")
    side = lax.axis_index("dp") % 2
    blocks = grad.reshape(slots // 2, 2, grad.shape[0] // slots, grad.shape[1])
    give = lax.dynamic_index_in_dim(blocks, 1 - side, 1, keepdims=False)
    kept = lax.dynamic_index_in_dim(blocks, side, 1, keepdims=False)
    return kept, lax.ppermute(give, "dp", [(i, i ^ 1) for i in range(slots)])


def pair_scatter(pair, *others):
    slots = lax.axis_size("dp")
    pairs = slots // 2
    own = lax.axis_index("dp") // 2
    kept, came = pair
    total = low(wide(kept) + wide(after(came, *others)))
    ahead = together(
        [
            lax.dynamic_index_in_dim(total, (own + step) % pairs, 0, keepdims=False)
            for step in range(pairs)
        ]
    )
    return [ahead[0]] + [
        lax.ppermute(ahead[step], "dp", [(i, (i + 2 * step) % slots) for i in range(slots)])
        for step in range(1, pairs)
    ]


def add_up(terms):
    total = terms[0]
    for term in terms[1:]:
        total = total + term
    return total


def per_device(
    tokens,
    cotangent,
    lengths,
    query_weight,
    key_weight,
    value_weight,
    out_weight,
    up_weight,
    down_weight,
    query_bias,
    value_bias,
    out_bias,
    norm1_gain,
    norm1_shift,
    up_bias,
    down_bias,
    norm2_gain,
    norm2_shift,
):
    rows, width = tokens.shape
    groups = lax.axis_size("tensor")
    position = lax.axis_index("tensor")
    head_cols = width // groups
    hidden_cols = FF // groups
    slot_len = lengths[0]
    col_start = position * head_cols
    hid_start = position * hidden_cols
    part = rows // CHUNKS
    cut = [slice(c * part, (c + 1) * part) for c in range(CHUNKS)]
    every = range(CHUNKS)
    run = part // 2
    limits = jnp.stack(
        [
            slot_len - ((position ^ p) * rows + c * part + side * run)
            for c in range(CHUNKS)
            for p, side in half_order()
        ]
    ).astype(jnp.int32)
    row_live = (position * rows + jnp.arange(rows, dtype=jnp.int32) < slot_len).astype(jnp.float32)[
        :, None
    ]
    bias_query = lax.dynamic_slice_in_dim(query_bias, col_start, head_cols)
    bias_value = lax.dynamic_slice_in_dim(value_bias, col_start, head_cols)
    bias_up = lax.dynamic_slice_in_dim(up_bias, hid_start, hidden_cols)
    bias_proj = jnp.concatenate([bias_query, jnp.zeros_like(bias_query), bias_value])

    proj_full = gather_weight(jnp.concatenate([query_weight, key_weight, value_weight], axis=1))
    out_full = gather_weight(out_weight)
    up_full = gather_weight(up_weight)
    down_full = gather_weight(down_weight)


    def lists(count):
        return ([None] * CHUNKS for _ in range(count))

    near, far, seq_tokens, projected = lists(4)
    before = ()
    for c in every:
        near[c] = gather_near(tokens[cut[c]], *before)
        far[c] = gather_far(near[c])
        before = far[c] or near[c]
        seq_tokens[c] = gathered(
            tokens[cut[c]], near[c], together(far[c], *projected[:c]) if far[c] else []
        )
        projected[c] = low(nn(seq_tokens[c], proj_full) + bias_proj)

    down_terms, up_terms = [], []
    context, lse, attn_low = lists(3)
    context[0], lse[0] = attend(0, projected, limits, run)
    attn_low[0] = low(nt(context[0], out_full))
    near[0] = scatter_near(attn_low[0])
    context[1], lse[1] = attend(1, [after(p, attn_low[0]) for p in projected], limits, run)
    far[0] = scatter_far(near[0], context[1])
    attn_low[1] = low(nt(after(context[1], *near[0][1]), out_full))

    def first_norm(c):
        attn_sum = scattered(near[c], far[c])
        result = norm_rows(wide(tokens[cut[c]]) + attn_sum + out_bias, norm1_gain, norm1_shift)
        return (*result, low(result[0]))

    def second_norm(c):
        ffn_sum = scattered(near[c], far[c])
        final, unit2, inverse2 = norm_rows(mid[c] + ffn_sum + down_bias, norm2_gain, norm2_shift)
        grad_final = wide(cotangent[cut[c]]) * row_live[cut[c]]
        grad_sum, gain_part, shift_part = norm_back(grad_final, unit2, inverse2, norm2_gain)
        return (
            low(final * row_live[cut[c]]),
            grad_sum,
            (gain_part, shift_part, jnp.sum(grad_sum, axis=0)),
            low(grad_sum),
        )

    def first_norm_back(c):
        mid_sum = scattered(near[c], far[c])
        grad_sum, gain_part, shift_part = norm_back(
            grad_sum2[c] + mid_sum, unit1[c], inverse1[c], norm1_gain
        )
        return (grad_sum, (gain_part, shift_part, jnp.sum(grad_sum, axis=0)), low(grad_sum))

    def turn(terms, norm, filler=None):
        near[1] = scatter_near(terms, *far[0])
        results = [norm(0), None]
        out = results[0][-1]
        if filler is not None:
            filler(0, (out,))
        far[1], near[0] = scatter_far_gather_near(near[1], out)
        if filler is not None:
            filler(1, tuple(near[1][1]))
        results[1] = norm(1)
        far[0] = gather_far(near[0], *down_terms[1:])
        whole = gathered(out, near[0], far[0])
        near[1] = gather_near(results[1][-1], *(far[0] or near[0]))
        return results, after(whole, results[1][-1])

    results, source = turn(attn_low[1], first_norm)
    mid, unit1, inverse1, mid_out = zip(*results)
    mid_seq, activ, slope, ffn_low = lists(4)
    mid_seq[0] = source
    activ[0], slope[0] = gate_and_slope(nn(source, up_full) + bias_up)
    far[1] = gather_far(near[1])
    ffn_low[0] = low(nt(after(activ[0], *near[1]), down_full))
    mid_seq[1] = gathered(mid_out[1], near[1], far[1])
    near[0] = scatter_near(ffn_low[0], *(far[1] or near[1]))
    activ[1], slope[1] = gate_and_slope(nn(after(mid_seq[1], ffn_low[0]), up_full) + bias_up)
    far[0] = scatter_far(near[0])
    ffn_low[1] = low(nt(after(activ[1], *near[0][1]), down_full))

    results, source = turn(ffn_low[1], second_norm)
    layer_out, grad_sum2, vec2, grad_out2 = zip(*results)
    grad_ffn, grad_pre, mid_low = lists(3)
    grad_ffn[0] = source
    grad_pre[0] = low(nn(source, down_full) * wide(slope[0]))
    far[1] = gather_far(near[1])
    mid_low[0] = low(nt(after(grad_pre[0], *near[1]), up_full))
    grad_ffn[1] = gathered(grad_out2[1], near[1], far[1])
    near[0] = scatter_near(mid_low[0], *(far[1] or near[1]))
    grad_pre[1] = low(nn(after(grad_ffn[1], mid_low[0]), down_full) * wide(slope[1]))
    far[0] = scatter_far(near[0])
    mid_low[1] = low(nt(after(grad_pre[1], *near[0][1]), up_full))

    def down_term(c, others):
        down_terms.append(tn(after(grad_ffn[c], *others), activ[c]))

    results, source = turn(mid_low[1], first_norm_back, down_term)
    down_grad = low(add_up(down_terms))
    down_part = scatter_weight(down_grad)
    up_bias_part = add_up([jnp.sum(wide(grad_pre[c]), axis=0) for c in every])
    grad_sum1, vec1, grad_out1 = zip(*results)
    grad_attn, grad_query = lists(2)
    grad_attn[0] = source
    grad_context = low(nn(after(source, down_grad), out_full))
    grad_query[0], *carry = attend_back(
        0, projected, context[0], grad_context, lse[0], limits, run, None
    )
    far[1] = gather_far(near[1], grad_query[0])
    up_terms.append(tn(after(mid_seq[0], grad_query[0], *near[1]), grad_pre[0]))
    up_terms.append(tn(after(mid_seq[1], up_terms[0]), grad_pre[1]))
    up_grad = low(add_up(up_terms))
    up_part = scatter_weight(up_grad)
    grad_attn[1] = gathered(
        grad_out1[1], near[1], together(far[1], up_terms[0]) if far[1] else []
    )
    grad_context = low(nn(after(grad_attn[1], up_grad), out_full))
    grad_query[1], *carry = attend_back(
        1, projected, context[1], grad_context, lse[1], limits, run, carry
    )
    size = part * groups
    grad_proj = [
        jnp.concatenate([grad_query[c]] + [a[c * size : (c + 1) * size] for a in carry], axis=1)
        for c in every
    ]
    tokens_low, tokens_grad = lists(2)

    def proj_term(i, *others):
        cols = slice(i * head_cols, (i + 1) * head_cols)
        return low(
            add_up([tn(after(seq_tokens[c], *others), grad_proj[c][:, cols]) for c in every])
        )

    tokens_low[0] = low(nt(after(grad_proj[0], up_grad, down_part), proj_full))
    near[0] = scatter_near(tokens_low[0])
    proj_grad, pair, proj_came = [None] * 3, [None] * 3, [None] * 3
    proj_grad[0] = proj_term(0, tokens_low[0])
    pair[0] = pair_exchange(proj_grad[0])
    proj_grad[1] = proj_term(1, proj_grad[0])
    pair[1] = pair_exchange(proj_grad[1])
    proj_came[0] = pair_scatter(pair[0], proj_grad[1])
    far[0] = scatter_far(near[0], proj_grad[1])
    tokens_low[1] = low(nt(after(grad_proj[1], pair[0][1], *near[0][1]), proj_full))
    near[1] = scatter_near(tokens_low[1], *far[0])
    proj_came[1] = pair_scatter(pair[1], tokens_low[1])
    proj_grad[2] = proj_term(2, tokens_low[1], pair[1][1], *far[0])
    pair[2] = pair_exchange(proj_grad[2])
    out_grad = low(add_up([tn(after(grad_attn[c], proj_grad[2]), context[c]) for c in every]))
    out_part = scatter_weight(out_grad)
    far[1] = scatter_far(near[1], out_grad)
    proj_came[2] = pair_scatter(pair[2], out_grad, *proj_came[0])
    for c in every:
        tokens_grad[c] = low(grad_sum1[c] + scattered(near[c], far[c]))
    out_part, up_part, down_part = map(wide, (out_part, up_part, down_part))
    proj_part = [add_up([wide(v) for v in came]) for came in proj_came]
    proj_bias = add_up([jnp.sum(wide(grad_proj[c]), axis=0) for c in every])
    (
        norm2_gain_grad,
        norm2_shift_grad,
        down_bias_grad,
        norm1_gain_grad,
        norm1_shift_grad,
        out_bias_grad,
        up_bias_grad,
        query_bias_grad,
        value_bias_grad,
    ) = total_of(
        [after(add_up([vec2[c][i] for c in every]), up_part) for i in range(3)]
        + [add_up([vec1[c][i] for c in every]) for i in range(3)]
        + [
            placed(up_bias_part, hid_start, FF),
            placed(proj_bias[:head_cols], col_start, width),
            placed(proj_bias[2 * head_cols :], col_start, width),
        ]
    )
    return (
        jnp.concatenate(layer_out, axis=0),
        jnp.concatenate(tokens_grad, axis=0),
        *proj_part,
        out_part,
        up_part,
        down_part,
        query_bias_grad,
        value_bias_grad,
        out_bias_grad,
        norm1_gain_grad,
        norm1_shift_grad,
        up_bias_grad,
        down_bias_grad,
        norm2_gain_grad,
        norm2_shift_grad,
    )


def solution(mesh):
    row = P(("dp", "tensor"), None)
    block = P("dp", "tensor")
    share = P(("dp", "tensor"))
    return jax.shard_map(
        per_device,
        mesh=mesh,
        in_specs=(row, row, P("dp")) + (block,) * 6 + (P(),) * 9,
        out_specs=(row, row) + (block,) * 6 + (share,) * 9,
        check_vma=False,
    )
```

```python
import jax
import jax.numpy as jnp
from jax import lax
from jax.experimental import pallas as pl
from jax.experimental.pallas import tpu as pltpu
from jax.sharding import PartitionSpec as P

HEADS = 16
HEAD_DIM = 128
FF = 8192
CHUNKS = 2

norm_eps = 1e-06
masked_score = -1e30
log2_e = 1.4426950408889634
score_scale = HEAD_DIM ** (-0.5)


def nt(left, right):
    return lax.dot_general(
        left, right, (((1,), (1,)), ((), ())), preferred_element_type=jnp.float32
    )


def nn(left, right):
    return lax.dot_general(
        left, right, (((1,), (0,)), ((), ())), preferred_element_type=jnp.float32
    )


def tn(left, right):
    return lax.dot_general(
        left, right, (((0,), (0,)), ((), ())), preferred_element_type=jnp.float32
    )


def low(value):
    return value.astype(jnp.bfloat16)


def wide(value):
    return value.astype(jnp.float32)


def half_order():
    size = lax.axis_size("tensor")
    if size != 4:
        return [(p, side) for p in range(size) for side in range(2)]
    return [(0, 0), (0, 1), (1, 1), (2, 0), (3, 0), (1, 0), (3, 1), (2, 1)]


def swap(value, bits):
    size = lax.axis_size("tensor")
    return lax.ppermute(value, "tensor", [(i, i ^ bits) for i in range(size)])


def after(value, *others):
    return lax.optimization_barrier((value, *others))[0]


def together(values, *others):
    values = tuple(values)
    return lax.optimization_barrier((*values, *others))[: len(values)]


def gather_near(own, *others):
    size = lax.axis_size("tensor")
    own = after(own, *others)
    return [swap(own, p) for p in range(1, 3 if size == 4 else size)]


def gather_far(near, *others):
    if lax.axis_size("tensor") != 4:
        return []
    half = near[0].shape[0] // 2
    near = together(near, *others)
    return [swap(near[0][:half], 2), swap(near[1][half:], 1)]


def gathered(own, near, far):
    if not far:
        return jnp.concatenate([own] + near, axis=0)
    half = own.shape[0] // 2
    first, second = near
    return jnp.concatenate(
        [own, first[half:], second[:half], far[0], first[:half], far[1], second[half:]], axis=0
    )


def scatter_near(terms, *others):
    size = lax.axis_size("tensor")
    rows = terms.shape[0] // size
    terms = after(terms, *others)
    if size != 4:
        return terms[:rows], [swap(terms[p * rows : (p + 1) * rows], p) for p in range(1, size)]
    return terms[: 2 * rows], [
        swap(terms[2 * rows : 3 * rows], 1),
        swap(terms[3 * rows :], 2),
    ]


def scatter_sums(near, *others):
    if lax.axis_size("tensor") != 4:
        return []
    kept, came = near
    first, second = together(came, *others)
    half = kept.shape[0] // 4
    lower = low(wide(second[:half]) + wide(kept[2 * half : 3 * half]))
    upper = low(wide(first[:half]) + wide(kept[3 * half :]))
    return together((lower, upper))


def scatter_far(near, *others):
    return [swap(value, p) for p, value in enumerate(scatter_sums(near, *others), 1)]


def scatter_far_gather_near(near, own):
    sums = scatter_sums(near)
    if not sums:
        return [], gather_near(own, *near[1])
    half = sums[0].shape[0]
    pieces = together([jnp.concatenate([value, own], axis=0) for value in sums])
    came = [swap(value, p) for p, value in enumerate(pieces, 1)]
    return [c[:half] for c in came], [c[half:] for c in came]


def scattered(near, far):
    kept, came = near
    if not far:
        return add_up([wide(kept)] + [wide(c) for c in came])
    half = kept.shape[0] // 4
    return jnp.concatenate(
        [
            wide(kept[:half]) + wide(came[0][half:]) + wide(far[1]),
            wide(kept[half : 2 * half]) + wide(came[1][half:]) + wide(far[0]),
        ],
        axis=0,
    )


def all_live(limits, run, count):
    full = limits[0] >= run
    for b in range(1, count):
        full = jnp.logical_and(full, limits[b] >= run)
    return full


def mask_dead(limits, run, count, ref, filler):
    for b in range(count):

        @pl.when(limits[b] < run)
        def _():
            rows = pl.ds(b * run, run)
            row = lax.broadcasted_iota(jnp.int32, (run, ref.shape[1]), 0)
            ref[rows, :] = jnp.where(row < limits[b], ref[rows, :], filler)


def attend(chunk, projected, limits, run):
    part = projected[0].shape[0]
    chunks = len(projected)
    cols = projected[0].shape[1] // 3
    heads = cols // HEAD_DIM
    keys_n = part * chunks
    count = keys_n // run
    block = min(1024, part)
    factor = score_scale * log2_e

    def kernel(lim, q_ref, *rest):
        k_refs, v_refs = rest[:chunks], rest[chunks : 2 * chunks]
        out_ref, lse_ref, s_ref = rest[2 * chunks :]
        q = q_ref[...]
        for c in range(chunks):
            s_ref[pl.ds(c * part, part), :] = nt(k_refs[c][...], q)

        @pl.when(jnp.logical_not(all_live(lim, run, count)))
        def _():
            mask_dead(lim, run, count, s_ref, masked_score)

        s = s_ref[...]
        top = jnp.max(s, axis=0, keepdims=True) * factor
        p = jnp.exp2(s * factor - top)
        total = jnp.sum(p, axis=0, keepdims=True)
        p = low(p)
        out = tn(v_refs[0][...], p[:part])
        for c in range(1, chunks):
            out = out + tn(v_refs[c][...], p[c * part : (c + 1) * part])
        out_ref[...] = low(jnp.transpose(out / total))
        lse_ref[0] = top + jnp.log2(total)

    key_spec = pl.BlockSpec((part, HEAD_DIM), lambda h, i, lim: (0, heads + h))
    value_spec = pl.BlockSpec((part, HEAD_DIM), lambda h, i, lim: (0, 2 * heads + h))
    row_spec = pl.BlockSpec((block, HEAD_DIM), lambda h, i, lim: (i, h))
    return pl.pallas_call(
        kernel,
        out_shape=(
            jax.ShapeDtypeStruct((part, cols), jnp.bfloat16),
            jax.ShapeDtypeStruct((heads, 1, part), jnp.float32),
        ),
        grid_spec=pltpu.PrefetchScalarGridSpec(
            num_scalar_prefetch=1,
            grid=(heads, part // block),
            in_specs=[row_spec] + [key_spec] * chunks + [value_spec] * chunks,
            out_specs=[row_spec, pl.BlockSpec((1, 1, block), lambda h, i, lim: (h, 0, i))],
            scratch_shapes=[pltpu.VMEM((keys_n, block), jnp.float32)],
        ),
        compiler_params=pltpu.CompilerParams(
            dimension_semantics=("arbitrary", "arbitrary"), vmem_limit_bytes=56 * 2**20
        ),
        cost_estimate=pl.CostEstimate(
            flops=8 * keys_n * part * cols,
            transcendentals=keys_n * part * heads,
            bytes_accessed=keys_n * cols * 4 + part * cols * 4,
        ),
        name="attend",
    )(limits, projected[chunk], *projected, *projected)


def attend_back(chunk, projected, context, grad, lse, limits, run, carry):
    part = projected[0].shape[0]
    chunks = len(projected)
    cols = projected[0].shape[1] // 3
    heads = cols // HEAD_DIM
    keys_n = part * chunks
    count = keys_n // run
    block = min(1024, part)
    steps = part // block
    factor = score_scale * log2_e
    last = chunk == chunks - 1

    def kernel(lim, q_ref, o_ref, do_ref, lse_ref, *rest):
        k_refs, v_refs = rest[:chunks], rest[chunks : 2 * chunks]
        rest = rest[2 * chunks :]
        if carry is not None:
            key_in, value_in = rest[:2]
            rest = rest[2:]
        dq_ref, dk_ref, dv_ref, p_ref, key_acc, value_acc = rest
        step = pl.program_id(1)

        @pl.when(step == 0)
        def _():
            if carry is None:
                key_acc[...] = jnp.zeros_like(key_acc)
                value_acc[...] = jnp.zeros_like(value_acc)
            else:
                key_acc[...] = key_in[...]
                value_acc[...] = value_in[...]

        q = q_ref[...]
        do = do_ref[...]
        lse = lse_ref[0]
        for c in range(chunks):
            p_ref[pl.ds(c * part, part), :] = jnp.exp2(nt(k_refs[c][...], q) * factor - lse)

        @pl.when(jnp.logical_not(all_live(lim, run, count)))
        def _():
            mask_dead(lim, run, count, p_ref, 0.0)

        inner = jnp.sum(jnp.transpose(wide(do) * wide(o_ref[...])), axis=0, keepdims=True)
        dq = None
        for c in range(chunks):
            rows = pl.ds(c * part, part)
            p = p_ref[rows, :]
            ds = low(p * (nt(v_refs[c][...], do) - inner))
            value_acc[rows, :] += nn(low(p), do)
            key_acc[rows, :] += nn(ds, q)
            term = tn(k_refs[c][...], ds)
            dq = term if dq is None else dq + term
        dq_ref[...] = low(jnp.transpose(dq * score_scale))

        @pl.when(step == steps - 1)
        def _():
            if last:
                dk_ref[...] = low(key_acc[...] * score_scale)
                dv_ref[...] = low(value_acc[...])
            else:
                dk_ref[...] = key_acc[...]
                dv_ref[...] = value_acc[...]

    key_spec = pl.BlockSpec((part, HEAD_DIM), lambda h, i, lim: (0, heads + h))
    value_spec = pl.BlockSpec((part, HEAD_DIM), lambda h, i, lim: (0, 2 * heads + h))
    row_spec = pl.BlockSpec((block, HEAD_DIM), lambda h, i, lim: (i, h))
    acc_spec = pl.BlockSpec((keys_n, HEAD_DIM), lambda h, i, lim: (0, h))
    acc_type = jnp.bfloat16 if last else jnp.float32
    acc_shape = jax.ShapeDtypeStruct((keys_n, cols), acc_type)
    return pl.pallas_call(
        kernel,
        out_shape=(jax.ShapeDtypeStruct((part, cols), jnp.bfloat16), acc_shape, acc_shape),
        grid_spec=pltpu.PrefetchScalarGridSpec(
            num_scalar_prefetch=1,
            grid=(heads, steps),
            in_specs=[
                row_spec,
                row_spec,
                row_spec,
                pl.BlockSpec((1, 1, block), lambda h, i, lim: (h, 0, i)),
            ]
            + [key_spec] * chunks
            + [value_spec] * chunks
            + ([] if carry is None else [acc_spec] * 2),
            out_specs=[row_spec, acc_spec, acc_spec],
            scratch_shapes=[
                pltpu.VMEM((keys_n, block), jnp.float32),
                pltpu.VMEM((keys_n, HEAD_DIM), jnp.float32),
                pltpu.VMEM((keys_n, HEAD_DIM), jnp.float32),
            ],
        ),
        compiler_params=pltpu.CompilerParams(
            dimension_semantics=("arbitrary", "arbitrary"), vmem_limit_bytes=56 * 2**20
        ),
        cost_estimate=pl.CostEstimate(
            flops=20 * keys_n * part * cols,
            transcendentals=keys_n * part * heads,
            bytes_accessed=keys_n * cols * 16 + part * cols * 8,
        ),
        name="attend_back",
    )(
        limits,
        projected[chunk],
        context,
        grad,
        lse,
        *projected,
        *projected,
        *(() if carry is None else carry),
    )


def norm_rows(value, gain, shift):
    centred = value - jnp.mean(value, axis=-1, keepdims=True)
    inverse = lax.rsqrt(jnp.mean(centred * centred, axis=-1, keepdims=True) + norm_eps)
    unit = centred * inverse
    return (unit * gain + shift, unit, inverse)


def norm_back(grad_out, unit, inverse, gain):
    grad_unit = grad_out * gain
    inner = jnp.mean(grad_unit * unit, axis=-1, keepdims=True)
    grad_in = inverse * (grad_unit - jnp.mean(grad_unit, axis=-1, keepdims=True) - unit * inner)
    return (grad_in, jnp.sum(grad_out * unit, axis=0), jnp.sum(grad_out, axis=0))


def gate_and_slope(pre):
    ratio = (2.0 / jnp.pi) ** 0.5
    square = pre * pre
    bent = jnp.tanh(ratio * (pre + 0.044715 * square * pre))
    half = 0.5 * (1.0 + bent)
    slope = half + 0.5 * pre * (1.0 - bent * bent) * (ratio * (1.0 + 3 * 0.044715 * square))
    return low(pre * half), low(slope)


def placed(part, start, total):
    return lax.dynamic_update_slice_in_dim(jnp.zeros((total,), jnp.float32), part, start, 0)


def total_of(vectors):
    slots, groups = lax.axis_size("dp"), lax.axis_size("tensor")
    slot, position = lax.axis_index("dp"), lax.axis_index("tensor")
    packed = jnp.concatenate([v.reshape(slots, groups, -1) for v in vectors], axis=2)

    def share(p):
        return lax.dynamic_index_in_dim(packed, position ^ p, 1, keepdims=False)

    total = add_up([share(0)] + [swap(share(p), p) for p in range(1, groups)])

    def ahead(step):
        return lax.dynamic_index_in_dim(total, (slot + step) % slots, 0, keepdims=False)

    total = add_up(
        [ahead(0)]
        + [
            lax.ppermute(ahead(step), "dp", [(i, (i + step) % slots) for i in range(slots)])
            for step in range(1, slots)
        ]
    )
    parts, at = [], 0
    for v in vectors:
        size = v.shape[0] // (slots * groups)
        parts.append(total[at : at + size])
        at += size
    return parts


def gather_weight(weight):
    return lax.all_gather(weight, "dp", axis=0, tiled=True)


def scatter_weight(grad):
    return lax.psum_scatter(grad, "dp", scatter_dimension=0, tiled=True)


def add_up(terms):
    total = terms[0]
    for term in terms[1:]:
        total = total + term
    return total


def per_device(
    tokens,
    cotangent,
    lengths,
    query_weight,
    key_weight,
    value_weight,
    out_weight,
    up_weight,
    down_weight,
    query_bias,
    value_bias,
    out_bias,
    norm1_gain,
    norm1_shift,
    up_bias,
    down_bias,
    norm2_gain,
    norm2_shift,
):
    rows, width = tokens.shape
    groups = lax.axis_size("tensor")
    position = lax.axis_index("tensor")
    head_cols = width // groups
    hidden_cols = FF // groups
    slot_len = lengths[0]
    col_start = position * head_cols
    hid_start = position * hidden_cols
    part = rows // CHUNKS
    cut = [slice(c * part, (c + 1) * part) for c in range(CHUNKS)]
    every = range(CHUNKS)
    run = part // 2
    limits = jnp.stack(
        [
            slot_len - ((position ^ p) * rows + c * part + side * run)
            for c in range(CHUNKS)
            for p, side in half_order()
        ]
    ).astype(jnp.int32)
    row_live = (position * rows + jnp.arange(rows, dtype=jnp.int32) < slot_len).astype(jnp.float32)[
        :, None
    ]
    bias_query = lax.dynamic_slice_in_dim(query_bias, col_start, head_cols)
    bias_value = lax.dynamic_slice_in_dim(value_bias, col_start, head_cols)
    bias_up = lax.dynamic_slice_in_dim(up_bias, hid_start, hidden_cols)
    bias_proj = jnp.concatenate([bias_query, jnp.zeros_like(bias_query), bias_value])

    proj_full = gather_weight(jnp.concatenate([query_weight, key_weight, value_weight], axis=1))
    out_full = gather_weight(out_weight)
    up_full = gather_weight(up_weight)
    down_full = gather_weight(down_weight)


    def lists(count):
        return ([None] * CHUNKS for _ in range(count))

    near, far, seq_tokens, projected = lists(4)
    before = ()
    for c in every:
        near[c] = gather_near(tokens[cut[c]], *before)
        far[c] = gather_far(near[c])
        before = far[c] or near[c]
        seq_tokens[c] = gathered(
            tokens[cut[c]], near[c], together(far[c], *projected[:c]) if far[c] else []
        )
        projected[c] = low(nn(seq_tokens[c], proj_full) + bias_proj)

    context, lse, attn_low = lists(3)
    context[0], lse[0] = attend(0, projected, limits, run)
    attn_low[0] = low(nt(context[0], out_full))
    near[0] = scatter_near(attn_low[0])
    context[1], lse[1] = attend(1, [after(p, attn_low[0]) for p in projected], limits, run)
    far[0] = scatter_far(near[0], context[1])
    attn_low[1] = low(nt(after(context[1], *near[0][1]), out_full))

    def first_norm(c):
        attn_sum = scattered(near[c], far[c])
        result = norm_rows(wide(tokens[cut[c]]) + attn_sum + out_bias, norm1_gain, norm1_shift)
        return (*result, low(result[0]))

    def second_norm(c):
        ffn_sum = scattered(near[c], far[c])
        final, unit2, inverse2 = norm_rows(mid[c] + ffn_sum + down_bias, norm2_gain, norm2_shift)
        grad_final = wide(cotangent[cut[c]]) * row_live[cut[c]]
        grad_sum, gain_part, shift_part = norm_back(grad_final, unit2, inverse2, norm2_gain)
        return (
            low(final * row_live[cut[c]]),
            grad_sum,
            (gain_part, shift_part, jnp.sum(grad_sum, axis=0)),
            low(grad_sum),
        )

    def first_norm_back(c):
        mid_sum = scattered(near[c], far[c])
        grad_sum, gain_part, shift_part = norm_back(
            grad_sum2[c] + mid_sum, unit1[c], inverse1[c], norm1_gain
        )
        return (grad_sum, (gain_part, shift_part, jnp.sum(grad_sum, axis=0)), low(grad_sum))

    def turn(terms, norm):
        near[1] = scatter_near(terms, *far[0])
        results = [norm(0), None]
        out = results[0][-1]
        far[1], near[0] = scatter_far_gather_near(near[1], out)
        results[1] = norm(1)
        far[0] = gather_far(near[0])
        whole = gathered(out, near[0], far[0])
        near[1] = gather_near(results[1][-1], *(far[0] or near[0]))
        return results, after(whole, results[1][-1])

    results, source = turn(attn_low[1], first_norm)
    mid, unit1, inverse1, mid_out = zip(*results)
    mid_seq, activ, slope, ffn_low = lists(4)
    mid_seq[0] = source
    activ[0], slope[0] = gate_and_slope(nn(source, up_full) + bias_up)
    far[1] = gather_far(near[1])
    ffn_low[0] = low(nt(after(activ[0], *near[1]), down_full))
    mid_seq[1] = gathered(mid_out[1], near[1], far[1])
    near[0] = scatter_near(ffn_low[0], *(far[1] or near[1]))
    activ[1], slope[1] = gate_and_slope(nn(after(mid_seq[1], ffn_low[0]), up_full) + bias_up)
    far[0] = scatter_far(near[0])
    ffn_low[1] = low(nt(after(activ[1], *near[0][1]), down_full))

    results, source = turn(ffn_low[1], second_norm)
    layer_out, grad_sum2, vec2, grad_out2 = zip(*results)
    grad_ffn, grad_pre, mid_low = lists(3)
    grad_ffn[0] = source
    grad_pre[0] = low(nn(source, down_full) * wide(slope[0]))
    far[1] = gather_far(near[1])
    mid_low[0] = low(nt(after(grad_pre[0], *near[1]), up_full))
    grad_ffn[1] = gathered(grad_out2[1], near[1], far[1])
    grad_sum1, vec1, grad_out1, grad_attn, grad_query, attn_near, attn_far = lists(7)
    down_terms, up_terms = lists(2)
    near[0] = scatter_near(mid_low[0], *(far[1] or near[1]))
    down_terms[1] = tn(after(grad_ffn[1], mid_low[0]), activ[1])
    far[0] = scatter_far(near[0])
    down_terms[0] = tn(after(grad_ffn[0], down_terms[1], *near[0][1]), activ[0])
    down_grad = low(add_up(down_terms[::-1]))
    down_part = scatter_weight(after(down_grad, *far[0]))
    grad_sum1[0], vec1[0], grad_out1[0] = first_norm_back(0)
    attn_near[0] = gather_near(grad_out1[0], *far[0])
    grad_pre[1] = low(
        nn(after(grad_ffn[1], down_grad, grad_out1[0]), down_full) * wide(slope[1])
    )
    attn_far[0] = gather_far(attn_near[0])
    mid_low[1] = low(nt(after(grad_pre[1], *attn_near[0]), up_full))
    grad_attn[0] = gathered(grad_out1[0], attn_near[0], attn_far[0])
    near[1] = scatter_near(mid_low[1], *(attn_far[0] or attn_near[0]))
    up_terms[0] = tn(
        after(mid_seq[0], mid_low[1], *(attn_far[0] or attn_near[0])), grad_pre[0]
    )
    far[1] = scatter_far(near[1])
    up_terms[1] = tn(after(mid_seq[1], up_terms[0], *near[1][1]), grad_pre[1])
    up_grad = low(add_up(up_terms))
    up_part = scatter_weight(after(up_grad, *far[1]))
    up_bias_part = add_up([jnp.sum(wide(grad_pre[c]), axis=0) for c in every])
    grad_sum1[1], vec1[1], grad_out1[1] = first_norm_back(1)
    attn_near[1] = gather_near(grad_out1[1], *far[1])
    grad_context = low(nn(after(grad_attn[0], up_grad, grad_out1[1]), out_full))
    grad_query[0], *carry = attend_back(
        0, projected, context[0], grad_context, lse[0], limits, run, None
    )
    attn_far[1] = gather_far(attn_near[1])
    out_term = tn(after(grad_attn[0], grad_query[0], *attn_near[1]), context[0])
    grad_attn[1] = gathered(grad_out1[1], attn_near[1], attn_far[1])
    out_grad = low(out_term + tn(grad_attn[1], context[1]))
    out_part = scatter_weight(out_grad)
    grad_context = low(nn(after(grad_attn[1], out_grad), out_full))
    grad_query[1], *carry = attend_back(
        1, projected, context[1], grad_context, lse[1], limits, run, carry
    )
    size = part * groups
    grad_proj = [
        jnp.concatenate([grad_query[c]] + [a[c * size : (c + 1) * size] for a in carry], axis=1)
        for c in every
    ]
    tokens_low, tokens_grad = lists(2)

    proj_terms = [None] * CHUNKS
    tokens_low[0] = low(nt(after(grad_proj[0], down_part), proj_full))
    near[0] = scatter_near(tokens_low[0])
    proj_terms[0] = tn(after(seq_tokens[0], tokens_low[0]), grad_proj[0])
    far[0] = scatter_far(near[0])
    tokens_low[1] = low(nt(after(grad_proj[1], proj_terms[0], *near[0][1]), proj_full))
    near[1] = scatter_near(tokens_low[1], *far[0])
    proj_terms[1] = tn(after(seq_tokens[1], tokens_low[1], *far[0]), grad_proj[1])
    proj_grad = low(add_up(proj_terms))
    proj_part = scatter_weight(after(proj_grad, *near[1][1]))
    far[1] = scatter_far(near[1])
    early = together((*(far[1] or near[1][1]), up_part))
    if far[1]:
        far[1] = early[:-1]
    up_part = early[-1]
    out_part = after(out_part, up_part)
    for c in every:
        tokens_grad[c] = low(grad_sum1[c] + scattered(near[c], far[c]))
    proj_part, out_part, up_part, down_part = map(wide, (proj_part, out_part, up_part, down_part))
    proj_bias = add_up([jnp.sum(wide(grad_proj[c]), axis=0) for c in every])
    (
        norm2_gain_grad,
        norm2_shift_grad,
        down_bias_grad,
        norm1_gain_grad,
        norm1_shift_grad,
        out_bias_grad,
        up_bias_grad,
        query_bias_grad,
        value_bias_grad,
    ) = total_of(
        [after(add_up([vec2[c][i] for c in every]), up_part) for i in range(3)]
        + [add_up([vec1[c][i] for c in every]) for i in range(3)]
        + [
            placed(up_bias_part, hid_start, FF),
            placed(proj_bias[:head_cols], col_start, width),
            placed(proj_bias[2 * head_cols :], col_start, width),
        ]
    )
    return (
        jnp.concatenate(layer_out, axis=0),
        jnp.concatenate(tokens_grad, axis=0),
        proj_part[:, :head_cols],
        proj_part[:, head_cols : 2 * head_cols],
        proj_part[:, 2 * head_cols :],
        out_part,
        up_part,
        down_part,
        query_bias_grad,
        value_bias_grad,
        out_bias_grad,
        norm1_gain_grad,
        norm1_shift_grad,
        up_bias_grad,
        down_bias_grad,
        norm2_gain_grad,
        norm2_shift_grad,
    )


def solution(mesh):
    row = P(("dp", "tensor"), None)
    block = P("dp", "tensor")
    share = P(("dp", "tensor"))
    return jax.shard_map(
        per_device,
        mesh=mesh,
        in_specs=(row, row, P("dp")) + (block,) * 6 + (P(),) * 9,
        out_specs=(row, row) + (block,) * 6 + (share,) * 9,
        check_vma=False,
    )
```

```python
import jax
import jax.numpy as jnp
from jax import lax
from jax.experimental import pallas as pl
from jax.experimental.pallas import tpu as pltpu
from jax.sharding import PartitionSpec as P

HEADS = 16
HEAD_DIM = 128
FF = 8192
CHUNKS = 2

norm_eps = 1e-06
masked_score = -1e30
log2_e = 1.4426950408889634
score_scale = HEAD_DIM ** (-0.5)


def nt(left, right):
    return lax.dot_general(
        left, right, (((1,), (1,)), ((), ())), preferred_element_type=jnp.float32
    )


def nn(left, right):
    return lax.dot_general(
        left, right, (((1,), (0,)), ((), ())), preferred_element_type=jnp.float32
    )


def tn(left, right):
    return lax.dot_general(
        left, right, (((0,), (0,)), ((), ())), preferred_element_type=jnp.float32
    )


def low(value):
    return value.astype(jnp.bfloat16)


def wide(value):
    return value.astype(jnp.float32)


def half_order():
    size = lax.axis_size("tensor")
    if size != 4:
        return [(p, side) for p in range(size) for side in range(2)]
    return [(0, 0), (0, 1), (1, 1), (2, 0), (3, 0), (1, 0), (3, 1), (2, 1)]


def swap(value, bits):
    size = lax.axis_size("tensor")
    return lax.ppermute(value, "tensor", [(i, i ^ bits) for i in range(size)])


def after(value, *others):
    return lax.optimization_barrier((value, *others))[0]


def together(values, *others):
    values = tuple(values)
    return lax.optimization_barrier((*values, *others))[: len(values)]


def gather_near(own, *others):
    size = lax.axis_size("tensor")
    own = after(own, *others)
    return [swap(own, p) for p in range(1, 3 if size == 4 else size)]


def gather_far(near, *others):
    if lax.axis_size("tensor") != 4:
        return []
    half = near[0].shape[0] // 2
    near = together(near, *others)
    return [swap(near[0][:half], 2), swap(near[1][half:], 1)]


def gathered(own, near, far):
    if not far:
        return jnp.concatenate([own] + near, axis=0)
    half = own.shape[0] // 2
    first, second = near
    return jnp.concatenate(
        [own, first[half:], second[:half], far[0], first[:half], far[1], second[half:]], axis=0
    )


def scatter_near(terms, *others):
    size = lax.axis_size("tensor")
    rows = terms.shape[0] // size
    terms = after(terms, *others)
    if size != 4:
        return terms[:rows], [swap(terms[p * rows : (p + 1) * rows], p) for p in range(1, size)]
    return terms[: 2 * rows], [
        swap(terms[2 * rows : 3 * rows], 1),
        swap(terms[3 * rows :], 2),
    ]


def scatter_sums(near, *others):
    if lax.axis_size("tensor") != 4:
        return []
    kept, came = near
    first, second = together(came, *others)
    half = kept.shape[0] // 4
    lower = low(wide(second[:half]) + wide(kept[2 * half : 3 * half]))
    upper = low(wide(first[:half]) + wide(kept[3 * half :]))
    return together((lower, upper))


def scatter_far(near, *others):
    return [swap(value, p) for p, value in enumerate(scatter_sums(near, *others), 1)]


def scatter_far_gather_near(near, own):
    sums = scatter_sums(near)
    if not sums:
        return [], gather_near(own, *near[1])
    half = sums[0].shape[0]
    pieces = together([jnp.concatenate([value, own], axis=0) for value in sums])
    came = [swap(value, p) for p, value in enumerate(pieces, 1)]
    return [c[:half] for c in came], [c[half:] for c in came]


def scattered(near, far):
    kept, came = near
    if not far:
        return add_up([wide(kept)] + [wide(c) for c in came])
    half = kept.shape[0] // 4
    return jnp.concatenate(
        [
            wide(kept[:half]) + wide(came[0][half:]) + wide(far[1]),
            wide(kept[half : 2 * half]) + wide(came[1][half:]) + wide(far[0]),
        ],
        axis=0,
    )


def all_live(limits, run, count):
    full = limits[0] >= run
    for b in range(1, count):
        full = jnp.logical_and(full, limits[b] >= run)
    return full


def mask_dead(limits, run, count, ref, filler):
    for b in range(count):

        @pl.when(limits[b] < run)
        def _():
            rows = pl.ds(b * run, run)
            row = lax.broadcasted_iota(jnp.int32, (run, ref.shape[1]), 0)
            ref[rows, :] = jnp.where(row < limits[b], ref[rows, :], filler)


def attend(chunk, projected, limits, run):
    part = projected[0].shape[0]
    chunks = len(projected)
    cols = projected[0].shape[1] // 3
    heads = cols // HEAD_DIM
    keys_n = part * chunks
    count = keys_n // run
    block = min(1024, part)
    factor = score_scale * log2_e

    def kernel(lim, q_ref, *rest):
        k_refs, v_refs = rest[:chunks], rest[chunks : 2 * chunks]
        out_ref, lse_ref, s_ref = rest[2 * chunks :]
        q = q_ref[...]
        for c in range(chunks):
            s_ref[pl.ds(c * part, part), :] = nt(k_refs[c][...], q)

        @pl.when(jnp.logical_not(all_live(lim, run, count)))
        def _():
            mask_dead(lim, run, count, s_ref, masked_score)

        s = s_ref[...]
        top = jnp.max(s, axis=0, keepdims=True) * factor
        p = jnp.exp2(s * factor - top)
        total = jnp.sum(p, axis=0, keepdims=True)
        p = low(p)
        out = tn(v_refs[0][...], p[:part])
        for c in range(1, chunks):
            out = out + tn(v_refs[c][...], p[c * part : (c + 1) * part])
        out_ref[...] = low(jnp.transpose(out / total))
        lse_ref[0] = top + jnp.log2(total)

    key_spec = pl.BlockSpec((part, HEAD_DIM), lambda h, i, lim: (0, heads + h))
    value_spec = pl.BlockSpec((part, HEAD_DIM), lambda h, i, lim: (0, 2 * heads + h))
    row_spec = pl.BlockSpec((block, HEAD_DIM), lambda h, i, lim: (i, h))
    return pl.pallas_call(
        kernel,
        out_shape=(
            jax.ShapeDtypeStruct((part, cols), jnp.bfloat16),
            jax.ShapeDtypeStruct((heads, 1, part), jnp.float32),
        ),
        grid_spec=pltpu.PrefetchScalarGridSpec(
            num_scalar_prefetch=1,
            grid=(heads, part // block),
            in_specs=[row_spec] + [key_spec] * chunks + [value_spec] * chunks,
            out_specs=[row_spec, pl.BlockSpec((1, 1, block), lambda h, i, lim: (h, 0, i))],
            scratch_shapes=[pltpu.VMEM((keys_n, block), jnp.float32)],
        ),
        compiler_params=pltpu.CompilerParams(
            dimension_semantics=("arbitrary", "arbitrary"), vmem_limit_bytes=56 * 2**20
        ),
        cost_estimate=pl.CostEstimate(
            flops=8 * keys_n * part * cols,
            transcendentals=keys_n * part * heads,
            bytes_accessed=keys_n * cols * 4 + part * cols * 4,
        ),
        name="attend",
    )(limits, projected[chunk], *projected, *projected)


def attend_back(chunk, projected, context, grad, lse, limits, run, carry):
    part = projected[0].shape[0]
    chunks = len(projected)
    cols = projected[0].shape[1] // 3
    heads = cols // HEAD_DIM
    keys_n = part * chunks
    count = keys_n // run
    block = min(1024, part)
    steps = part // block
    factor = score_scale * log2_e
    last = chunk == chunks - 1

    def kernel(lim, q_ref, o_ref, do_ref, lse_ref, *rest):
        k_refs, v_refs = rest[:chunks], rest[chunks : 2 * chunks]
        rest = rest[2 * chunks :]
        if carry is not None:
            key_in, value_in = rest[:2]
            rest = rest[2:]
        dq_ref, dk_ref, dv_ref, p_ref, key_acc, value_acc = rest
        step = pl.program_id(1)

        @pl.when(step == 0)
        def _():
            if carry is None:
                key_acc[...] = jnp.zeros_like(key_acc)
                value_acc[...] = jnp.zeros_like(value_acc)
            else:
                key_acc[...] = key_in[...]
                value_acc[...] = value_in[...]

        q = q_ref[...]
        do = do_ref[...]
        lse = lse_ref[0]
        for c in range(chunks):
            p_ref[pl.ds(c * part, part), :] = jnp.exp2(nt(k_refs[c][...], q) * factor - lse)

        @pl.when(jnp.logical_not(all_live(lim, run, count)))
        def _():
            mask_dead(lim, run, count, p_ref, 0.0)

        inner = jnp.sum(jnp.transpose(wide(do) * wide(o_ref[...])), axis=0, keepdims=True)
        dq = None
        for c in range(chunks):
            rows = pl.ds(c * part, part)
            p = p_ref[rows, :]
            ds = low(p * (nt(v_refs[c][...], do) - inner))
            value_acc[rows, :] += nn(low(p), do)
            key_acc[rows, :] += nn(ds, q)
            term = tn(k_refs[c][...], ds)
            dq = term if dq is None else dq + term
        dq_ref[...] = low(jnp.transpose(dq * score_scale))

        @pl.when(step == steps - 1)
        def _():
            if last:
                dk_ref[...] = low(key_acc[...] * score_scale)
                dv_ref[...] = low(value_acc[...])
            else:
                dk_ref[...] = key_acc[...]
                dv_ref[...] = value_acc[...]

    key_spec = pl.BlockSpec((part, HEAD_DIM), lambda h, i, lim: (0, heads + h))
    value_spec = pl.BlockSpec((part, HEAD_DIM), lambda h, i, lim: (0, 2 * heads + h))
    row_spec = pl.BlockSpec((block, HEAD_DIM), lambda h, i, lim: (i, h))
    acc_spec = pl.BlockSpec((keys_n, HEAD_DIM), lambda h, i, lim: (0, h))
    acc_type = jnp.bfloat16 if last else jnp.float32
    acc_shape = jax.ShapeDtypeStruct((keys_n, cols), acc_type)
    return pl.pallas_call(
        kernel,
        out_shape=(jax.ShapeDtypeStruct((part, cols), jnp.bfloat16), acc_shape, acc_shape),
        grid_spec=pltpu.PrefetchScalarGridSpec(
            num_scalar_prefetch=1,
            grid=(heads, steps),
            in_specs=[
                row_spec,
                row_spec,
                row_spec,
                pl.BlockSpec((1, 1, block), lambda h, i, lim: (h, 0, i)),
            ]
            + [key_spec] * chunks
            + [value_spec] * chunks
            + ([] if carry is None else [acc_spec] * 2),
            out_specs=[row_spec, acc_spec, acc_spec],
            scratch_shapes=[
                pltpu.VMEM((keys_n, block), jnp.float32),
                pltpu.VMEM((keys_n, HEAD_DIM), jnp.float32),
                pltpu.VMEM((keys_n, HEAD_DIM), jnp.float32),
            ],
        ),
        compiler_params=pltpu.CompilerParams(
            dimension_semantics=("arbitrary", "arbitrary"), vmem_limit_bytes=56 * 2**20
        ),
        cost_estimate=pl.CostEstimate(
            flops=20 * keys_n * part * cols,
            transcendentals=keys_n * part * heads,
            bytes_accessed=keys_n * cols * 16 + part * cols * 8,
        ),
        name="attend_back",
    )(
        limits,
        projected[chunk],
        context,
        grad,
        lse,
        *projected,
        *projected,
        *(() if carry is None else carry),
    )


def norm_rows(value, gain, shift):
    centred = value - jnp.mean(value, axis=-1, keepdims=True)
    inverse = lax.rsqrt(jnp.mean(centred * centred, axis=-1, keepdims=True) + norm_eps)
    unit = centred * inverse
    return (unit * gain + shift, unit, inverse)


def norm_back(grad_out, unit, inverse, gain):
    grad_unit = grad_out * gain
    inner = jnp.mean(grad_unit * unit, axis=-1, keepdims=True)
    grad_in = inverse * (grad_unit - jnp.mean(grad_unit, axis=-1, keepdims=True) - unit * inner)
    return (grad_in, jnp.sum(grad_out * unit, axis=0), jnp.sum(grad_out, axis=0))


def gate_and_slope(pre):
    ratio = (2.0 / jnp.pi) ** 0.5
    square = pre * pre
    bent = jnp.tanh(ratio * (pre + 0.044715 * square * pre))
    half = 0.5 * (1.0 + bent)
    slope = half + 0.5 * pre * (1.0 - bent * bent) * (ratio * (1.0 + 3 * 0.044715 * square))
    return low(pre * half), low(slope)


def placed(part, start, total):
    return lax.dynamic_update_slice_in_dim(jnp.zeros((total,), jnp.float32), part, start, 0)


def total_of(vectors):
    slots, groups = lax.axis_size("dp"), lax.axis_size("tensor")
    slot, position = lax.axis_index("dp"), lax.axis_index("tensor")
    packed = jnp.concatenate([v.reshape(slots, groups, -1) for v in vectors], axis=2)

    def share(p):
        return lax.dynamic_index_in_dim(packed, position ^ p, 1, keepdims=False)

    total = add_up([share(0)] + [swap(share(p), p) for p in range(1, groups)])

    def ahead(step):
        return lax.dynamic_index_in_dim(total, (slot + step) % slots, 0, keepdims=False)

    total = add_up(
        [ahead(0)]
        + [
            lax.ppermute(ahead(step), "dp", [(i, (i + step) % slots) for i in range(slots)])
            for step in range(1, slots)
        ]
    )
    parts, at = [], 0
    for v in vectors:
        size = v.shape[0] // (slots * groups)
        parts.append(total[at : at + size])
        at += size
    return parts


def gather_weight(weight):
    return lax.all_gather(weight, "dp", axis=0, tiled=True)


def scatter_weight(grad):
    return lax.psum_scatter(grad, "dp", scatter_dimension=0, tiled=True)


def add_up(terms):
    total = terms[0]
    for term in terms[1:]:
        total = total + term
    return total


def per_device(
    tokens,
    cotangent,
    lengths,
    query_weight,
    key_weight,
    value_weight,
    out_weight,
    up_weight,
    down_weight,
    query_bias,
    value_bias,
    out_bias,
    norm1_gain,
    norm1_shift,
    up_bias,
    down_bias,
    norm2_gain,
    norm2_shift,
):
    rows, width = tokens.shape
    groups = lax.axis_size("tensor")
    position = lax.axis_index("tensor")
    head_cols = width // groups
    hidden_cols = FF // groups
    slot_len = lengths[0]
    col_start = position * head_cols
    hid_start = position * hidden_cols
    part = rows // CHUNKS
    cut = [slice(c * part, (c + 1) * part) for c in range(CHUNKS)]
    every = range(CHUNKS)
    run = part // 2
    limits = jnp.stack(
        [
            slot_len - ((position ^ p) * rows + c * part + side * run)
            for c in range(CHUNKS)
            for p, side in half_order()
        ]
    ).astype(jnp.int32)
    row_live = (position * rows + jnp.arange(rows, dtype=jnp.int32) < slot_len).astype(jnp.float32)[
        :, None
    ]
    bias_query = lax.dynamic_slice_in_dim(query_bias, col_start, head_cols)
    bias_value = lax.dynamic_slice_in_dim(value_bias, col_start, head_cols)
    bias_up = lax.dynamic_slice_in_dim(up_bias, hid_start, hidden_cols)
    bias_proj = jnp.concatenate([bias_query, jnp.zeros_like(bias_query), bias_value])

    proj_full = gather_weight(jnp.concatenate([query_weight, key_weight, value_weight], axis=1))
    out_full = gather_weight(out_weight)
    up_full = gather_weight(up_weight)
    down_full = gather_weight(down_weight)


    def lists(count):
        return ([None] * CHUNKS for _ in range(count))

    near, far, seq_tokens, projected = lists(4)
    before = ()
    for c in every:
        near[c] = gather_near(tokens[cut[c]], *before)
        far[c] = gather_far(near[c])
        before = far[c] or near[c]
        seq_tokens[c] = gathered(
            tokens[cut[c]], near[c], together(far[c], *projected[:c]) if far[c] else []
        )
        projected[c] = low(nn(seq_tokens[c], proj_full) + bias_proj)

    context, lse, attn_low = lists(3)
    context[0], lse[0] = attend(0, projected, limits, run)
    attn_low[0] = low(nt(context[0], out_full))
    near[0] = scatter_near(attn_low[0])
    context[1], lse[1] = attend(1, [after(p, attn_low[0]) for p in projected], limits, run)
    far[0] = scatter_far(near[0], context[1])
    attn_low[1] = low(nt(after(context[1], *near[0][1]), out_full))

    def first_norm(c):
        attn_sum = scattered(near[c], far[c])
        result = norm_rows(wide(tokens[cut[c]]) + attn_sum + out_bias, norm1_gain, norm1_shift)
        return (*result, low(result[0]))

    def second_norm(c):
        ffn_sum = scattered(near[c], far[c])
        final, unit2, inverse2 = norm_rows(mid[c] + ffn_sum + down_bias, norm2_gain, norm2_shift)
        grad_final = wide(cotangent[cut[c]]) * row_live[cut[c]]
        grad_sum, gain_part, shift_part = norm_back(grad_final, unit2, inverse2, norm2_gain)
        return (
            low(final * row_live[cut[c]]),
            grad_sum,
            (gain_part, shift_part, jnp.sum(grad_sum, axis=0)),
            low(grad_sum),
        )

    def first_norm_back(c):
        mid_sum = scattered(near[c], far[c])
        grad_sum, gain_part, shift_part = norm_back(
            grad_sum2[c] + mid_sum, unit1[c], inverse1[c], norm1_gain
        )
        return (grad_sum, (gain_part, shift_part, jnp.sum(grad_sum, axis=0)), low(grad_sum))

    def turn(terms, norm):
        near[1] = scatter_near(terms, *far[0])
        results = [norm(0), None]
        out = results[0][-1]
        far[1], near[0] = scatter_far_gather_near(near[1], out)
        results[1] = norm(1)
        far[0] = gather_far(near[0])
        whole = gathered(out, near[0], far[0])
        near[1] = gather_near(results[1][-1], *(far[0] or near[0]))
        return results, after(whole, results[1][-1])

    results, source = turn(attn_low[1], first_norm)
    mid, unit1, inverse1, mid_out = zip(*results)
    mid_seq, activ, slope, ffn_low = lists(4)
    mid_seq[0] = source
    activ[0], slope[0] = gate_and_slope(nn(source, up_full) + bias_up)
    far[1] = gather_far(near[1])
    ffn_low[0] = low(nt(after(activ[0], *near[1]), down_full))
    mid_seq[1] = gathered(mid_out[1], near[1], far[1])
    near[0] = scatter_near(ffn_low[0], *(far[1] or near[1]))
    activ[1], slope[1] = gate_and_slope(nn(after(mid_seq[1], ffn_low[0]), up_full) + bias_up)
    far[0] = scatter_far(near[0])
    ffn_low[1] = low(nt(after(activ[1], *near[0][1]), down_full))

    results, source = turn(ffn_low[1], second_norm)
    layer_out, grad_sum2, vec2, grad_out2 = zip(*results)
    grad_ffn, grad_pre, mid_low = lists(3)
    grad_ffn[0] = source
    grad_pre[0] = low(nn(source, down_full) * wide(slope[0]))
    far[1] = gather_far(near[1])
    mid_low[0] = low(nt(after(grad_pre[0], *near[1]), up_full))
    grad_ffn[1] = gathered(grad_out2[1], near[1], far[1])
    grad_sum1, vec1, grad_out1, grad_attn, grad_query, attn_near, attn_far = lists(7)
    down_terms, up_terms = lists(2)
    near[0] = scatter_near(mid_low[0], *(far[1] or near[1]))
    down_terms[1] = tn(after(grad_ffn[1], mid_low[0]), activ[1])
    far[0] = scatter_far(near[0])
    down_terms[0] = tn(after(grad_ffn[0], down_terms[1], *near[0][1]), activ[0])
    down_grad = low(add_up(down_terms[::-1]))
    down_part = scatter_weight(after(down_grad, *far[0]))
    grad_sum1[0], vec1[0], grad_out1[0] = first_norm_back(0)
    attn_near[0] = gather_near(grad_out1[0], *far[0])
    grad_pre[1] = low(
        nn(after(grad_ffn[1], down_grad, grad_out1[0]), down_full) * wide(slope[1])
    )
    attn_far[0] = gather_far(attn_near[0])
    mid_low[1] = low(nt(after(grad_pre[1], *attn_near[0]), up_full))
    grad_attn[0] = gathered(grad_out1[0], attn_near[0], attn_far[0])
    near[1] = scatter_near(mid_low[1], *(attn_far[0] or attn_near[0]))
    up_terms[0] = tn(
        after(mid_seq[0], mid_low[1], *(attn_far[0] or attn_near[0])), grad_pre[0]
    )
    far[1] = scatter_far(near[1])
    up_terms[1] = tn(after(mid_seq[1], up_terms[0], *near[1][1]), grad_pre[1])
    up_grad = low(add_up(up_terms))
    up_part = scatter_weight(after(up_grad, *far[1]))
    up_bias_part = add_up([jnp.sum(wide(grad_pre[c]), axis=0) for c in every])
    grad_sum1[1], vec1[1], grad_out1[1] = first_norm_back(1)
    attn_near[1] = gather_near(grad_out1[1], *far[1])
    grad_context = low(nn(after(grad_attn[0], up_grad, grad_out1[1]), out_full))
    grad_query[0], *carry = attend_back(
        0, projected, context[0], grad_context, lse[0], limits, run, None
    )
    attn_far[1] = gather_far(attn_near[1])
    out_term = tn(after(grad_attn[0], grad_query[0], *attn_near[1]), context[0])
    grad_attn[1] = gathered(
        grad_out1[1], attn_near[1], together(attn_far[1], out_term) if attn_far[1] else []
    )
    out_grad = low(out_term + tn(grad_attn[1], context[1]))
    out_part = scatter_weight(out_grad)
    grad_context = low(nn(after(grad_attn[1], out_grad), out_full))
    grad_query[1], *carry = attend_back(
        1, projected, context[1], grad_context, lse[1], limits, run, carry
    )
    size = part * groups
    grad_proj = [
        jnp.concatenate([grad_query[c]] + [a[c * size : (c + 1) * size] for a in carry], axis=1)
        for c in every
    ]
    tokens_low, tokens_grad = lists(2)

    proj_terms = [None] * CHUNKS
    tokens_low[0] = low(nt(after(grad_proj[0], down_part), proj_full))
    near[0] = scatter_near(tokens_low[0])
    proj_terms[1] = tn(after(seq_tokens[1], tokens_low[0]), grad_proj[1])
    proj_terms[0] = tn(after(seq_tokens[0], proj_terms[1], *near[0][1]), grad_proj[0])
    far[0] = scatter_far(near[0])
    proj_grad = low(proj_terms[1] + proj_terms[0])
    proj_part = scatter_weight(proj_grad)
    tokens_low[1] = low(nt(after(grad_proj[1], proj_grad), proj_full))
    near[1] = scatter_near(tokens_low[1], *far[0])
    far[1] = scatter_far(near[1])
    early = together((*(far[1] or near[1][1]), up_part))
    if far[1]:
        far[1] = early[:-1]
    up_part = early[-1]
    out_part = after(out_part, up_part)
    for c in every:
        tokens_grad[c] = low(grad_sum1[c] + scattered(near[c], far[c]))
    proj_part, out_part, up_part, down_part = map(wide, (proj_part, out_part, up_part, down_part))
    proj_bias = add_up(
        [jnp.sum(wide(after(grad_proj[c], tokens_low[1])), axis=0) for c in every]
    )
    (
        norm2_gain_grad,
        norm2_shift_grad,
        down_bias_grad,
        norm1_gain_grad,
        norm1_shift_grad,
        out_bias_grad,
        up_bias_grad,
        query_bias_grad,
        value_bias_grad,
    ) = total_of(
        [after(add_up([vec2[c][i] for c in every]), up_part) for i in range(3)]
        + [add_up([vec1[c][i] for c in every]) for i in range(3)]
        + [
            placed(up_bias_part, hid_start, FF),
            placed(proj_bias[:head_cols], col_start, width),
            placed(proj_bias[2 * head_cols :], col_start, width),
        ]
    )
    return (
        jnp.concatenate(layer_out, axis=0),
        jnp.concatenate(tokens_grad, axis=0),
        proj_part[:, :head_cols],
        proj_part[:, head_cols : 2 * head_cols],
        proj_part[:, 2 * head_cols :],
        out_part,
        up_part,
        down_part,
        query_bias_grad,
        value_bias_grad,
        out_bias_grad,
        norm1_gain_grad,
        norm1_shift_grad,
        up_bias_grad,
        down_bias_grad,
        norm2_gain_grad,
        norm2_shift_grad,
    )


def solution(mesh):
    row = P(("dp", "tensor"), None)
    block = P("dp", "tensor")
    share = P(("dp", "tensor"))
    return jax.shard_map(
        per_device,
        mesh=mesh,
        in_specs=(row, row, P("dp")) + (block,) * 6 + (P(),) * 9,
        out_specs=(row, row) + (block,) * 6 + (share,) * 9,
        check_vma=False,
    )
```

```python
import jax
import jax.numpy as jnp
from jax import lax
from jax.experimental import pallas as pl
from jax.experimental.pallas import tpu as pltpu
from jax.sharding import PartitionSpec as P

HEADS = 16
HEAD_DIM = 128
FF = 8192
CHUNKS = 2

norm_eps = 1e-06
masked_score = -1e30
log2_e = 1.4426950408889634
score_scale = HEAD_DIM ** (-0.5)


def nt(left, right):
    return lax.dot_general(
        left, right, (((1,), (1,)), ((), ())), preferred_element_type=jnp.float32
    )


def nn(left, right):
    return lax.dot_general(
        left, right, (((1,), (0,)), ((), ())), preferred_element_type=jnp.float32
    )


def tn(left, right):
    return lax.dot_general(
        left, right, (((0,), (0,)), ((), ())), preferred_element_type=jnp.float32
    )


def low(value):
    return value.astype(jnp.bfloat16)


def wide(value):
    return value.astype(jnp.float32)


def half_order():
    size = lax.axis_size("tensor")
    if size != 4:
        return [(p, side) for p in range(size) for side in range(2)]
    return [(0, 0), (0, 1), (1, 1), (2, 0), (3, 0), (1, 0), (3, 1), (2, 1)]


def swap(value, bits):
    size = lax.axis_size("tensor")
    return lax.ppermute(value, "tensor", [(i, i ^ bits) for i in range(size)])


def after(value, *others):
    return lax.optimization_barrier((value, *others))[0]


def together(values, *others):
    values = tuple(values)
    return lax.optimization_barrier((*values, *others))[: len(values)]


def gather_near(own, *others):
    size = lax.axis_size("tensor")
    own = after(own, *others)
    return [swap(own, p) for p in range(1, 3 if size == 4 else size)]


def gather_far(near, *others):
    if lax.axis_size("tensor") != 4:
        return []
    half = near[0].shape[0] // 2
    near = together(near, *others)
    return [swap(near[0][:half], 2), swap(near[1][half:], 1)]


def gathered(own, near, far):
    if not far:
        return jnp.concatenate([own] + near, axis=0)
    half = own.shape[0] // 2
    first, second = near
    return jnp.concatenate(
        [own, first[half:], second[:half], far[0], first[:half], far[1], second[half:]], axis=0
    )


def scatter_near(terms, *others):
    size = lax.axis_size("tensor")
    rows = terms.shape[0] // size
    terms = after(terms, *others)
    if size != 4:
        return terms[:rows], [swap(terms[p * rows : (p + 1) * rows], p) for p in range(1, size)]
    return terms[: 2 * rows], [
        swap(terms[2 * rows : 3 * rows], 1),
        swap(terms[3 * rows :], 2),
    ]


def scatter_sums(near, *others):
    if lax.axis_size("tensor") != 4:
        return []
    kept, came = near
    first, second = together(came, *others)
    half = kept.shape[0] // 4
    lower = low(wide(second[:half]) + wide(kept[2 * half : 3 * half]))
    upper = low(wide(first[:half]) + wide(kept[3 * half :]))
    return together((lower, upper))


def scatter_far(near, *others):
    return [swap(value, p) for p, value in enumerate(scatter_sums(near, *others), 1)]


def scatter_far_gather_near(near, own):
    sums = scatter_sums(near)
    if not sums:
        return [], gather_near(own, *near[1])
    half = sums[0].shape[0]
    pieces = together([jnp.concatenate([value, own], axis=0) for value in sums])
    came = [swap(value, p) for p, value in enumerate(pieces, 1)]
    return [c[:half] for c in came], [c[half:] for c in came]


def scattered(near, far):
    kept, came = near
    if not far:
        return add_up([wide(kept)] + [wide(c) for c in came])
    half = kept.shape[0] // 4
    return jnp.concatenate(
        [
            wide(kept[:half]) + wide(came[0][half:]) + wide(far[1]),
            wide(kept[half : 2 * half]) + wide(came[1][half:]) + wide(far[0]),
        ],
        axis=0,
    )


def all_live(limits, run, count):
    full = limits[0] >= run
    for b in range(1, count):
        full = jnp.logical_and(full, limits[b] >= run)
    return full


def mask_dead(limits, run, count, ref, filler):
    for b in range(count):

        @pl.when(limits[b] < run)
        def _():
            rows = pl.ds(b * run, run)
            row = lax.broadcasted_iota(jnp.int32, (run, ref.shape[1]), 0)
            ref[rows, :] = jnp.where(row < limits[b], ref[rows, :], filler)


def attend(chunk, projected, limits, run):
    part = projected[0].shape[0]
    chunks = len(projected)
    cols = projected[0].shape[1] // 3
    heads = cols // HEAD_DIM
    keys_n = part * chunks
    count = keys_n // run
    block = min(1024, part)
    factor = score_scale * log2_e

    def kernel(lim, q_ref, *rest):
        k_refs, v_refs = rest[:chunks], rest[chunks : 2 * chunks]
        out_ref, lse_ref, s_ref = rest[2 * chunks :]
        q = q_ref[...]
        for c in range(chunks):
            s_ref[pl.ds(c * part, part), :] = nt(k_refs[c][...], q)

        @pl.when(jnp.logical_not(all_live(lim, run, count)))
        def _():
            mask_dead(lim, run, count, s_ref, masked_score)

        s = s_ref[...]
        top = jnp.max(s, axis=0, keepdims=True) * factor
        p = jnp.exp2(s * factor - top)
        total = jnp.sum(p, axis=0, keepdims=True)
        p = low(p)
        out = tn(v_refs[0][...], p[:part])
        for c in range(1, chunks):
            out = out + tn(v_refs[c][...], p[c * part : (c + 1) * part])
        out_ref[...] = low(jnp.transpose(out / total))
        lse_ref[0] = top + jnp.log2(total)

    key_spec = pl.BlockSpec((part, HEAD_DIM), lambda h, i, lim: (0, heads + h))
    value_spec = pl.BlockSpec((part, HEAD_DIM), lambda h, i, lim: (0, 2 * heads + h))
    row_spec = pl.BlockSpec((block, HEAD_DIM), lambda h, i, lim: (i, h))
    return pl.pallas_call(
        kernel,
        out_shape=(
            jax.ShapeDtypeStruct((part, cols), jnp.bfloat16),
            jax.ShapeDtypeStruct((heads, 1, part), jnp.float32),
        ),
        grid_spec=pltpu.PrefetchScalarGridSpec(
            num_scalar_prefetch=1,
            grid=(heads, part // block),
            in_specs=[row_spec] + [key_spec] * chunks + [value_spec] * chunks,
            out_specs=[row_spec, pl.BlockSpec((1, 1, block), lambda h, i, lim: (h, 0, i))],
            scratch_shapes=[pltpu.VMEM((keys_n, block), jnp.float32)],
        ),
        compiler_params=pltpu.CompilerParams(
            dimension_semantics=("arbitrary", "arbitrary"), vmem_limit_bytes=56 * 2**20
        ),
        cost_estimate=pl.CostEstimate(
            flops=8 * keys_n * part * cols,
            transcendentals=keys_n * part * heads,
            bytes_accessed=keys_n * cols * 4 + part * cols * 4,
        ),
        name="attend",
    )(limits, projected[chunk], *projected, *projected)


def attend_back(chunk, projected, context, grad, lse, limits, run, carry):
    part = projected[0].shape[0]
    chunks = len(projected)
    cols = projected[0].shape[1] // 3
    heads = cols // HEAD_DIM
    keys_n = part * chunks
    count = keys_n // run
    block = min(1024, part)
    steps = part // block
    factor = score_scale * log2_e
    last = chunk == chunks - 1

    def kernel(lim, q_ref, o_ref, do_ref, lse_ref, *rest):
        k_refs, v_refs = rest[:chunks], rest[chunks : 2 * chunks]
        rest = rest[2 * chunks :]
        if carry is not None:
            key_in, value_in = rest[:2]
            rest = rest[2:]
        dq_ref, dk_ref, dv_ref, p_ref, key_acc, value_acc = rest
        step = pl.program_id(1)

        @pl.when(step == 0)
        def _():
            if carry is None:
                key_acc[...] = jnp.zeros_like(key_acc)
                value_acc[...] = jnp.zeros_like(value_acc)
            else:
                key_acc[...] = key_in[...]
                value_acc[...] = value_in[...]

        q = q_ref[...]
        do = do_ref[...]
        lse = lse_ref[0]
        for c in range(chunks):
            p_ref[pl.ds(c * part, part), :] = jnp.exp2(nt(k_refs[c][...], q) * factor - lse)

        @pl.when(jnp.logical_not(all_live(lim, run, count)))
        def _():
            mask_dead(lim, run, count, p_ref, 0.0)

        inner = jnp.sum(jnp.transpose(wide(do) * wide(o_ref[...])), axis=0, keepdims=True)
        dq = None
        for c in range(chunks):
            rows = pl.ds(c * part, part)
            p = p_ref[rows, :]
            ds = low(p * (nt(v_refs[c][...], do) - inner))
            value_acc[rows, :] += nn(low(p), do)
            key_acc[rows, :] += nn(ds, q)
            term = tn(k_refs[c][...], ds)
            dq = term if dq is None else dq + term
        dq_ref[...] = low(jnp.transpose(dq * score_scale))

        @pl.when(step == steps - 1)
        def _():
            if last:
                dk_ref[...] = low(key_acc[...] * score_scale)
                dv_ref[...] = low(value_acc[...])
            else:
                dk_ref[...] = key_acc[...]
                dv_ref[...] = value_acc[...]

    key_spec = pl.BlockSpec((part, HEAD_DIM), lambda h, i, lim: (0, heads + h))
    value_spec = pl.BlockSpec((part, HEAD_DIM), lambda h, i, lim: (0, 2 * heads + h))
    row_spec = pl.BlockSpec((block, HEAD_DIM), lambda h, i, lim: (i, h))
    acc_spec = pl.BlockSpec((keys_n, HEAD_DIM), lambda h, i, lim: (0, h))
    acc_type = jnp.bfloat16 if last else jnp.float32
    acc_shape = jax.ShapeDtypeStruct((keys_n, cols), acc_type)
    return pl.pallas_call(
        kernel,
        out_shape=(jax.ShapeDtypeStruct((part, cols), jnp.bfloat16), acc_shape, acc_shape),
        grid_spec=pltpu.PrefetchScalarGridSpec(
            num_scalar_prefetch=1,
            grid=(heads, steps),
            in_specs=[
                row_spec,
                row_spec,
                row_spec,
                pl.BlockSpec((1, 1, block), lambda h, i, lim: (h, 0, i)),
            ]
            + [key_spec] * chunks
            + [value_spec] * chunks
            + ([] if carry is None else [acc_spec] * 2),
            out_specs=[row_spec, acc_spec, acc_spec],
            scratch_shapes=[
                pltpu.VMEM((keys_n, block), jnp.float32),
                pltpu.VMEM((keys_n, HEAD_DIM), jnp.float32),
                pltpu.VMEM((keys_n, HEAD_DIM), jnp.float32),
            ],
        ),
        compiler_params=pltpu.CompilerParams(
            dimension_semantics=("arbitrary", "arbitrary"), vmem_limit_bytes=56 * 2**20
        ),
        cost_estimate=pl.CostEstimate(
            flops=20 * keys_n * part * cols,
            transcendentals=keys_n * part * heads,
            bytes_accessed=keys_n * cols * 16 + part * cols * 8,
        ),
        name="attend_back",
    )(
        limits,
        projected[chunk],
        context,
        grad,
        lse,
        *projected,
        *projected,
        *(() if carry is None else carry),
    )


def norm_rows(value, gain, shift):
    centred = value - jnp.mean(value, axis=-1, keepdims=True)
    inverse = lax.rsqrt(jnp.mean(centred * centred, axis=-1, keepdims=True) + norm_eps)
    unit = centred * inverse
    return (unit * gain + shift, unit, inverse)


def norm_back(grad_out, unit, inverse, gain):
    grad_unit = grad_out * gain
    inner = jnp.mean(grad_unit * unit, axis=-1, keepdims=True)
    grad_in = inverse * (grad_unit - jnp.mean(grad_unit, axis=-1, keepdims=True) - unit * inner)
    return (grad_in, jnp.sum(grad_out * unit, axis=0), jnp.sum(grad_out, axis=0))


def gate_and_slope(pre):
    ratio = (2.0 / jnp.pi) ** 0.5
    square = pre * pre
    bent = jnp.tanh(ratio * (pre + 0.044715 * square * pre))
    half = 0.5 * (1.0 + bent)
    slope = half + 0.5 * pre * (1.0 - bent * bent) * (ratio * (1.0 + 3 * 0.044715 * square))
    return low(pre * half), low(slope)


def placed(part, start, total):
    return lax.dynamic_update_slice_in_dim(jnp.zeros((total,), jnp.float32), part, start, 0)


def total_of(vectors):
    slots, groups = lax.axis_size("dp"), lax.axis_size("tensor")
    slot, position = lax.axis_index("dp"), lax.axis_index("tensor")
    packed = jnp.concatenate([v.reshape(slots, groups, -1) for v in vectors], axis=2)

    def share(p):
        return lax.dynamic_index_in_dim(packed, position ^ p, 1, keepdims=False)

    total = add_up([share(0)] + [swap(share(p), p) for p in range(1, groups)])

    def ahead(step):
        return lax.dynamic_index_in_dim(total, (slot + step) % slots, 0, keepdims=False)

    total = add_up(
        [ahead(0)]
        + [
            lax.ppermute(ahead(step), "dp", [(i, (i + step) % slots) for i in range(slots)])
            for step in range(1, slots)
        ]
    )
    parts, at = [], 0
    for v in vectors:
        size = v.shape[0] // (slots * groups)
        parts.append(total[at : at + size])
        at += size
    return parts


def gather_weight(weight):
    return lax.all_gather(weight, "dp", axis=0, tiled=True)


def scatter_weight(grad):
    return lax.psum_scatter(grad, "dp", scatter_dimension=0, tiled=True)


def add_up(terms):
    total = terms[0]
    for term in terms[1:]:
        total = total + term
    return total


def per_device(
    tokens,
    cotangent,
    lengths,
    query_weight,
    key_weight,
    value_weight,
    out_weight,
    up_weight,
    down_weight,
    query_bias,
    value_bias,
    out_bias,
    norm1_gain,
    norm1_shift,
    up_bias,
    down_bias,
    norm2_gain,
    norm2_shift,
):
    rows, width = tokens.shape
    groups = lax.axis_size("tensor")
    position = lax.axis_index("tensor")
    head_cols = width // groups
    hidden_cols = FF // groups
    slot_len = lengths[0]
    col_start = position * head_cols
    hid_start = position * hidden_cols
    part = rows // CHUNKS
    cut = [slice(c * part, (c + 1) * part) for c in range(CHUNKS)]
    every = range(CHUNKS)
    run = part // 2
    limits = jnp.stack(
        [
            slot_len - ((position ^ p) * rows + c * part + side * run)
            for c in range(CHUNKS)
            for p, side in half_order()
        ]
    ).astype(jnp.int32)
    row_live = (position * rows + jnp.arange(rows, dtype=jnp.int32) < slot_len).astype(jnp.float32)[
        :, None
    ]
    bias_query = lax.dynamic_slice_in_dim(query_bias, col_start, head_cols)
    bias_value = lax.dynamic_slice_in_dim(value_bias, col_start, head_cols)
    bias_up = lax.dynamic_slice_in_dim(up_bias, hid_start, hidden_cols)
    bias_proj = jnp.concatenate([bias_query, jnp.zeros_like(bias_query), bias_value])

    proj_full = gather_weight(jnp.concatenate([query_weight, key_weight, value_weight], axis=1))
    out_full = gather_weight(out_weight)
    up_full = gather_weight(up_weight)
    down_full = gather_weight(down_weight)


    def lists(count):
        return ([None] * CHUNKS for _ in range(count))

    near, far, seq_tokens, projected = lists(4)
    before = ()
    for c in every:
        near[c] = gather_near(tokens[cut[c]], *before)
        far[c] = gather_far(near[c])
        before = far[c] or near[c]
        seq_tokens[c] = gathered(
            tokens[cut[c]], near[c], together(far[c], *projected[:c]) if far[c] else []
        )
        projected[c] = low(nn(seq_tokens[c], proj_full) + bias_proj)

    context, lse, attn_low = lists(3)
    context[0], lse[0] = attend(0, projected, limits, run)
    attn_low[0] = low(nt(context[0], out_full))
    near[0] = scatter_near(attn_low[0])
    context[1], lse[1] = attend(1, [after(p, attn_low[0]) for p in projected], limits, run)
    far[0] = scatter_far(near[0], context[1])
    attn_low[1] = low(nt(after(context[1], *near[0][1]), out_full))

    def first_norm(c):
        attn_sum = scattered(near[c], far[c])
        result = norm_rows(wide(tokens[cut[c]]) + attn_sum + out_bias, norm1_gain, norm1_shift)
        return (*result, low(result[0]))

    def second_norm(c):
        ffn_sum = scattered(near[c], far[c])
        final, unit2, inverse2 = norm_rows(mid[c] + ffn_sum + down_bias, norm2_gain, norm2_shift)
        grad_final = wide(cotangent[cut[c]]) * row_live[cut[c]]
        grad_sum, gain_part, shift_part = norm_back(grad_final, unit2, inverse2, norm2_gain)
        return (
            low(final * row_live[cut[c]]),
            grad_sum,
            (gain_part, shift_part, jnp.sum(grad_sum, axis=0)),
            low(grad_sum),
        )

    def first_norm_back(c):
        mid_sum = scattered(near[c], far[c])
        grad_sum, gain_part, shift_part = norm_back(
            grad_sum2[c] + mid_sum, unit1[c], inverse1[c], norm1_gain
        )
        return (grad_sum, (gain_part, shift_part, jnp.sum(grad_sum, axis=0)), low(grad_sum))

    def turn(terms, norm):
        near[1] = scatter_near(terms, *far[0])
        results = [norm(0), None]
        out = results[0][-1]
        far[1], near[0] = scatter_far_gather_near(near[1], out)
        results[1] = norm(1)
        far[0] = gather_far(near[0])
        whole = gathered(out, near[0], far[0])
        near[1] = gather_near(results[1][-1], *(far[0] or near[0]))
        return results, after(whole, results[1][-1])

    results, source = turn(attn_low[1], first_norm)
    mid, unit1, inverse1, mid_out = zip(*results)
    mid_seq, activ, slope, ffn_low = lists(4)
    mid_seq[0] = source
    activ[0], slope[0] = gate_and_slope(nn(source, up_full) + bias_up)
    far[1] = gather_far(near[1])
    ffn_low[0] = low(nt(after(activ[0], *near[1]), down_full))
    mid_seq[1] = gathered(mid_out[1], near[1], far[1])
    near[0] = scatter_near(ffn_low[0], *(far[1] or near[1]))
    activ[1], slope[1] = gate_and_slope(nn(after(mid_seq[1], ffn_low[0]), up_full) + bias_up)
    far[0] = scatter_far(near[0])
    ffn_low[1] = low(nt(after(activ[1], *near[0][1]), down_full))

    results, source = turn(ffn_low[1], second_norm)
    layer_out, grad_sum2, vec2, grad_out2 = zip(*results)
    grad_ffn, grad_pre, mid_low = lists(3)
    grad_ffn[0] = source
    grad_pre[0] = low(nn(source, down_full) * wide(slope[0]))
    far[1] = gather_far(near[1])
    mid_low[0] = low(nt(after(grad_pre[0], *near[1]), up_full))
    grad_ffn[1] = gathered(grad_out2[1], near[1], far[1])
    grad_sum1, vec1, grad_out1, grad_attn, grad_query, attn_near, attn_far = lists(7)
    down_terms, up_terms = lists(2)
    near[0] = scatter_near(mid_low[0], *(far[1] or near[1]))
    down_terms[1] = tn(after(grad_ffn[1], mid_low[0]), activ[1])
    far[0] = scatter_far(near[0])
    down_terms[0] = tn(after(grad_ffn[0], down_terms[1], *near[0][1]), activ[0])
    down_grad = low(add_up(down_terms[::-1]))
    down_part = scatter_weight(after(down_grad, *far[0]))
    grad_sum1[0], vec1[0], grad_out1[0] = first_norm_back(0)
    attn_near[0] = gather_near(grad_out1[0], *far[0])
    grad_pre[1] = low(
        nn(after(grad_ffn[1], down_grad, grad_out1[0]), down_full) * wide(slope[1])
    )
    attn_far[0] = gather_far(attn_near[0])
    mid_low[1] = low(nt(after(grad_pre[1], *attn_near[0]), up_full))
    grad_attn[0] = gathered(grad_out1[0], attn_near[0], attn_far[0])
    near[1] = scatter_near(mid_low[1], *(attn_far[0] or attn_near[0]))
    up_terms[0] = tn(
        after(mid_seq[0], mid_low[1], *(attn_far[0] or attn_near[0])), grad_pre[0]
    )
    far[1] = scatter_far(near[1])
    up_terms[1] = tn(after(mid_seq[1], up_terms[0], *near[1][1]), grad_pre[1])
    up_grad = low(add_up(up_terms))
    up_part = scatter_weight(after(up_grad, *far[1]))
    up_bias_part = add_up([jnp.sum(wide(grad_pre[c]), axis=0) for c in every])
    grad_sum1[1], vec1[1], grad_out1[1] = first_norm_back(1)
    attn_near[1] = gather_near(grad_out1[1], *far[1])
    grad_context = low(nn(after(grad_attn[0], up_grad, grad_out1[1]), out_full))
    grad_query[0], *carry = attend_back(
        0, projected, context[0], grad_context, lse[0], limits, run, None
    )
    attn_far[1] = gather_far(attn_near[1])
    out_term = tn(after(grad_attn[0], grad_query[0], *attn_near[1]), context[0])
    grad_attn[1] = gathered(
        grad_out1[1], attn_near[1], together(attn_far[1], out_term) if attn_far[1] else []
    )
    out_grad = low(out_term + tn(grad_attn[1], context[1]))
    out_part = scatter_weight(out_grad)
    grad_context = low(nn(after(grad_attn[1], out_grad), out_full))
    grad_query[1], *carry = attend_back(
        1, projected, context[1], grad_context, lse[1], limits, run, carry
    )
    size = part * groups
    grad_proj = [
        jnp.concatenate([grad_query[c]] + [a[c * size : (c + 1) * size] for a in carry], axis=1)
        for c in every
    ]
    tokens_low, tokens_grad = lists(2)

    proj_terms = [None] * CHUNKS
    proj_terms[0] = tn(after(seq_tokens[0], down_part), grad_proj[0])
    proj_terms[1] = tn(after(seq_tokens[1], proj_terms[0]), grad_proj[1])
    proj_grad = low(add_up(proj_terms))
    proj_part = scatter_weight(proj_grad)
    tokens_low[0] = low(nt(after(grad_proj[0], proj_grad), proj_full))
    near[0] = scatter_near(tokens_low[0])
    tokens_low[1] = low(nt(after(grad_proj[1], tokens_low[0]), proj_full))
    far[0] = scatter_far(near[0], tokens_low[1])
    near[1] = scatter_near(tokens_low[1], *(far[0] or near[0][1]))
    proj_bias = add_up(
        [jnp.sum(wide(after(grad_proj[c], tokens_low[1])), axis=0) for c in every]
    )
    sums = total_of(
        [after(add_up([vec2[c][i] for c in every]), up_part) for i in range(3)]
        + [add_up([vec1[c][i] for c in every]) for i in range(3)]
        + [
            placed(up_bias_part, hid_start, FF),
            placed(proj_bias[:head_cols], col_start, width),
            placed(proj_bias[2 * head_cols :], col_start, width),
        ]
    )
    out_part = after(out_part, up_part)
    far[1] = scatter_far(near[1], sums[0])
    for c in every:
        tokens_grad[c] = low(grad_sum1[c] + scattered(near[c], far[c]))
    proj_part, out_part, up_part, down_part = map(wide, (proj_part, out_part, up_part, down_part))
    (
        norm2_gain_grad,
        norm2_shift_grad,
        down_bias_grad,
        norm1_gain_grad,
        norm1_shift_grad,
        out_bias_grad,
        up_bias_grad,
        query_bias_grad,
        value_bias_grad,
    ) = sums
    return (
        jnp.concatenate(layer_out, axis=0),
        jnp.concatenate(tokens_grad, axis=0),
        proj_part[:, :head_cols],
        proj_part[:, head_cols : 2 * head_cols],
        proj_part[:, 2 * head_cols :],
        out_part,
        up_part,
        down_part,
        query_bias_grad,
        value_bias_grad,
        out_bias_grad,
        norm1_gain_grad,
        norm1_shift_grad,
        up_bias_grad,
        down_bias_grad,
        norm2_gain_grad,
        norm2_shift_grad,
    )


def solution(mesh):
    row = P(("dp", "tensor"), None)
    block = P("dp", "tensor")
    share = P(("dp", "tensor"))
    return jax.shard_map(
        per_device,
        mesh=mesh,
        in_specs=(row, row, P("dp")) + (block,) * 6 + (P(),) * 9,
        out_specs=(row, row) + (block,) * 6 + (share,) * 9,
        check_vma=False,
    )
```

```python
import jax
import jax.numpy as jnp
from jax import lax
from jax.experimental import pallas as pl
from jax.experimental.pallas import tpu as pltpu
from jax.sharding import PartitionSpec as P

HEADS = 16
HEAD_DIM = 128
FF = 8192
CHUNKS = 2

norm_eps = 1e-06
masked_score = -1e30
log2_e = 1.4426950408889634
score_scale = HEAD_DIM ** (-0.5)


def nt(left, right):
    return lax.dot_general(
        left, right, (((1,), (1,)), ((), ())), preferred_element_type=jnp.float32
    )


def nn(left, right):
    return lax.dot_general(
        left, right, (((1,), (0,)), ((), ())), preferred_element_type=jnp.float32
    )


def tn(left, right):
    return lax.dot_general(
        left, right, (((0,), (0,)), ((), ())), preferred_element_type=jnp.float32
    )


def low(value):
    return value.astype(jnp.bfloat16)


def wide(value):
    return value.astype(jnp.float32)


def half_order():
    size = lax.axis_size("tensor")
    if size != 4:
        return [(p, side) for p in range(size) for side in range(2)]
    return [(0, 0), (0, 1), (1, 1), (2, 0), (3, 0), (1, 0), (3, 1), (2, 1)]


def swap(value, bits):
    size = lax.axis_size("tensor")
    return lax.ppermute(value, "tensor", [(i, i ^ bits) for i in range(size)])


def after(value, *others):
    return lax.optimization_barrier((value, *others))[0]


def together(values, *others):
    values = tuple(values)
    return lax.optimization_barrier((*values, *others))[: len(values)]


def gather_near(own, *others):
    size = lax.axis_size("tensor")
    own = after(own, *others)
    return [swap(own, p) for p in range(1, 3 if size == 4 else size)]


def gather_far(near, *others):
    if lax.axis_size("tensor") != 4:
        return []
    half = near[0].shape[0] // 2
    near = together(near, *others)
    return [swap(near[0][:half], 2), swap(near[1][half:], 1)]


def gathered(own, near, far):
    if not far:
        return jnp.concatenate([own] + near, axis=0)
    half = own.shape[0] // 2
    first, second = near
    return jnp.concatenate(
        [own, first[half:], second[:half], far[0], first[:half], far[1], second[half:]], axis=0
    )


def scatter_near(terms, *others):
    size = lax.axis_size("tensor")
    rows = terms.shape[0] // size
    terms = after(terms, *others)
    if size != 4:
        return terms[:rows], [swap(terms[p * rows : (p + 1) * rows], p) for p in range(1, size)]
    return terms[: 2 * rows], [
        swap(terms[2 * rows : 3 * rows], 1),
        swap(terms[3 * rows :], 2),
    ]


def scatter_sums(near, *others):
    if lax.axis_size("tensor") != 4:
        return []
    kept, came = near
    first, second = together(came, *others)
    half = kept.shape[0] // 4
    lower = low(wide(second[:half]) + wide(kept[2 * half : 3 * half]))
    upper = low(wide(first[:half]) + wide(kept[3 * half :]))
    return together((lower, upper))


def scatter_far(near, *others):
    return [swap(value, p) for p, value in enumerate(scatter_sums(near, *others), 1)]


def scatter_far_gather_near(near, own):
    sums = scatter_sums(near)
    if not sums:
        return [], gather_near(own, *near[1])
    half = sums[0].shape[0]
    pieces = together([jnp.concatenate([value, own], axis=0) for value in sums])
    came = [swap(value, p) for p, value in enumerate(pieces, 1)]
    return [c[:half] for c in came], [c[half:] for c in came]


def scattered(near, far):
    kept, came = near
    if not far:
        return add_up([wide(kept)] + [wide(c) for c in came])
    half = kept.shape[0] // 4
    return jnp.concatenate(
        [
            wide(kept[:half]) + wide(came[0][half:]) + wide(far[1]),
            wide(kept[half : 2 * half]) + wide(came[1][half:]) + wide(far[0]),
        ],
        axis=0,
    )


def all_live(limits, run, count):
    full = limits[0] >= run
    for b in range(1, count):
        full = jnp.logical_and(full, limits[b] >= run)
    return full


def mask_dead(limits, run, count, ref, filler):
    for b in range(count):

        @pl.when(limits[b] < run)
        def _():
            rows = pl.ds(b * run, run)
            row = lax.broadcasted_iota(jnp.int32, (run, ref.shape[1]), 0)
            ref[rows, :] = jnp.where(row < limits[b], ref[rows, :], filler)


def attend(chunk, projected, limits, run):
    part = projected[0].shape[0]
    chunks = len(projected)
    cols = projected[0].shape[1] // 3
    heads = cols // HEAD_DIM
    keys_n = part * chunks
    count = keys_n // run
    block = min(1024, part)
    factor = score_scale * log2_e

    def kernel(lim, q_ref, *rest):
        k_refs, v_refs = rest[:chunks], rest[chunks : 2 * chunks]
        out_ref, lse_ref, s_ref = rest[2 * chunks :]
        q = q_ref[...]
        for c in range(chunks):
            s_ref[pl.ds(c * part, part), :] = nt(k_refs[c][...], q)

        @pl.when(jnp.logical_not(all_live(lim, run, count)))
        def _():
            mask_dead(lim, run, count, s_ref, masked_score)

        s = s_ref[...]
        top = jnp.max(s, axis=0, keepdims=True) * factor
        p = jnp.exp2(s * factor - top)
        total = jnp.sum(p, axis=0, keepdims=True)
        p = low(p)
        out = tn(v_refs[0][...], p[:part])
        for c in range(1, chunks):
            out = out + tn(v_refs[c][...], p[c * part : (c + 1) * part])
        out_ref[...] = low(jnp.transpose(out / total))
        lse_ref[0] = top + jnp.log2(total)

    key_spec = pl.BlockSpec((part, HEAD_DIM), lambda h, i, lim: (0, heads + h))
    value_spec = pl.BlockSpec((part, HEAD_DIM), lambda h, i, lim: (0, 2 * heads + h))
    row_spec = pl.BlockSpec((block, HEAD_DIM), lambda h, i, lim: (i, h))
    return pl.pallas_call(
        kernel,
        out_shape=(
            jax.ShapeDtypeStruct((part, cols), jnp.bfloat16),
            jax.ShapeDtypeStruct((heads, 1, part), jnp.float32),
        ),
        grid_spec=pltpu.PrefetchScalarGridSpec(
            num_scalar_prefetch=1,
            grid=(heads, part // block),
            in_specs=[row_spec] + [key_spec] * chunks + [value_spec] * chunks,
            out_specs=[row_spec, pl.BlockSpec((1, 1, block), lambda h, i, lim: (h, 0, i))],
            scratch_shapes=[pltpu.VMEM((keys_n, block), jnp.float32)],
        ),
        compiler_params=pltpu.CompilerParams(
            dimension_semantics=("arbitrary", "arbitrary"), vmem_limit_bytes=56 * 2**20
        ),
        cost_estimate=pl.CostEstimate(
            flops=8 * keys_n * part * cols,
            transcendentals=keys_n * part * heads,
            bytes_accessed=keys_n * cols * 4 + part * cols * 4,
        ),
        name="attend",
    )(limits, projected[chunk], *projected, *projected)


def attend_back(chunk, projected, context, grad, lse, limits, run, carry):
    part = projected[0].shape[0]
    chunks = len(projected)
    cols = projected[0].shape[1] // 3
    heads = cols // HEAD_DIM
    keys_n = part * chunks
    count = keys_n // run
    block = min(1024, part)
    steps = part // block
    factor = score_scale * log2_e
    last = chunk == chunks - 1

    def kernel(lim, q_ref, o_ref, do_ref, lse_ref, *rest):
        k_refs, v_refs = rest[:chunks], rest[chunks : 2 * chunks]
        rest = rest[2 * chunks :]
        if carry is not None:
            key_in, value_in = rest[:2]
            rest = rest[2:]
        dq_ref, dk_ref, dv_ref, p_ref, key_acc, value_acc = rest
        step = pl.program_id(1)

        @pl.when(step == 0)
        def _():
            if carry is None:
                key_acc[...] = jnp.zeros_like(key_acc)
                value_acc[...] = jnp.zeros_like(value_acc)
            else:
                key_acc[...] = key_in[...]
                value_acc[...] = value_in[...]

        q = q_ref[...]
        do = do_ref[...]
        lse = lse_ref[0]
        for c in range(chunks):
            p_ref[pl.ds(c * part, part), :] = jnp.exp2(nt(k_refs[c][...], q) * factor - lse)

        @pl.when(jnp.logical_not(all_live(lim, run, count)))
        def _():
            mask_dead(lim, run, count, p_ref, 0.0)

        inner = jnp.sum(jnp.transpose(wide(do) * wide(o_ref[...])), axis=0, keepdims=True)
        dq = None
        for c in range(chunks):
            rows = pl.ds(c * part, part)
            p = p_ref[rows, :]
            ds = low(p * (nt(v_refs[c][...], do) - inner))
            value_acc[rows, :] += nn(low(p), do)
            key_acc[rows, :] += nn(ds, q)
            term = tn(k_refs[c][...], ds)
            dq = term if dq is None else dq + term
        dq_ref[...] = low(jnp.transpose(dq * score_scale))

        @pl.when(step == steps - 1)
        def _():
            if last:
                dk_ref[...] = low(key_acc[...] * score_scale)
                dv_ref[...] = low(value_acc[...])
            else:
                dk_ref[...] = key_acc[...]
                dv_ref[...] = value_acc[...]

    key_spec = pl.BlockSpec((part, HEAD_DIM), lambda h, i, lim: (0, heads + h))
    value_spec = pl.BlockSpec((part, HEAD_DIM), lambda h, i, lim: (0, 2 * heads + h))
    row_spec = pl.BlockSpec((block, HEAD_DIM), lambda h, i, lim: (i, h))
    acc_spec = pl.BlockSpec((keys_n, HEAD_DIM), lambda h, i, lim: (0, h))
    acc_type = jnp.bfloat16 if last else jnp.float32
    acc_shape = jax.ShapeDtypeStruct((keys_n, cols), acc_type)
    return pl.pallas_call(
        kernel,
        out_shape=(jax.ShapeDtypeStruct((part, cols), jnp.bfloat16), acc_shape, acc_shape),
        grid_spec=pltpu.PrefetchScalarGridSpec(
            num_scalar_prefetch=1,
            grid=(heads, steps),
            in_specs=[
                row_spec,
                row_spec,
                row_spec,
                pl.BlockSpec((1, 1, block), lambda h, i, lim: (h, 0, i)),
            ]
            + [key_spec] * chunks
            + [value_spec] * chunks
            + ([] if carry is None else [acc_spec] * 2),
            out_specs=[row_spec, acc_spec, acc_spec],
            scratch_shapes=[
                pltpu.VMEM((keys_n, block), jnp.float32),
                pltpu.VMEM((keys_n, HEAD_DIM), jnp.float32),
                pltpu.VMEM((keys_n, HEAD_DIM), jnp.float32),
            ],
        ),
        compiler_params=pltpu.CompilerParams(
            dimension_semantics=("arbitrary", "arbitrary"), vmem_limit_bytes=56 * 2**20
        ),
        cost_estimate=pl.CostEstimate(
            flops=20 * keys_n * part * cols,
            transcendentals=keys_n * part * heads,
            bytes_accessed=keys_n * cols * 16 + part * cols * 8,
        ),
        name="attend_back",
    )(
        limits,
        projected[chunk],
        context,
        grad,
        lse,
        *projected,
        *projected,
        *(() if carry is None else carry),
    )


def norm_rows(value, gain, shift):
    centred = value - jnp.mean(value, axis=-1, keepdims=True)
    inverse = lax.rsqrt(jnp.mean(centred * centred, axis=-1, keepdims=True) + norm_eps)
    unit = centred * inverse
    return (unit * gain + shift, unit, inverse)


def norm_back(grad_out, unit, inverse, gain):
    grad_unit = grad_out * gain
    inner = jnp.mean(grad_unit * unit, axis=-1, keepdims=True)
    grad_in = inverse * (grad_unit - jnp.mean(grad_unit, axis=-1, keepdims=True) - unit * inner)
    return (grad_in, jnp.sum(grad_out * unit, axis=0), jnp.sum(grad_out, axis=0))


def gate_and_slope(pre):
    ratio = (2.0 / jnp.pi) ** 0.5
    square = pre * pre
    bent = jnp.tanh(ratio * (pre + 0.044715 * square * pre))
    half = 0.5 * (1.0 + bent)
    slope = half + 0.5 * pre * (1.0 - bent * bent) * (ratio * (1.0 + 3 * 0.044715 * square))
    return low(pre * half), low(slope)


def placed(part, start, total):
    return lax.dynamic_update_slice_in_dim(jnp.zeros((total,), jnp.float32), part, start, 0)


def total_of(vectors):
    slots, groups = lax.axis_size("dp"), lax.axis_size("tensor")
    slot, position = lax.axis_index("dp"), lax.axis_index("tensor")
    packed = jnp.concatenate([v.reshape(slots, groups, -1) for v in vectors], axis=2)

    def share(p):
        return lax.dynamic_index_in_dim(packed, position ^ p, 1, keepdims=False)

    total = add_up([share(0)] + [swap(share(p), p) for p in range(1, groups)])

    def ahead(step):
        return lax.dynamic_index_in_dim(total, (slot + step) % slots, 0, keepdims=False)

    total = add_up(
        [ahead(0)]
        + [
            lax.ppermute(ahead(step), "dp", [(i, (i + step) % slots) for i in range(slots)])
            for step in range(1, slots)
        ]
    )
    parts, at = [], 0
    for v in vectors:
        size = v.shape[0] // (slots * groups)
        parts.append(total[at : at + size])
        at += size
    return parts


def gather_weight(weight):
    return lax.all_gather(weight, "dp", axis=0, tiled=True)


def scatter_weight(grad):
    return lax.psum_scatter(grad, "dp", scatter_dimension=0, tiled=True)


def add_up(terms):
    total = terms[0]
    for term in terms[1:]:
        total = total + term
    return total


def per_device(
    tokens,
    cotangent,
    lengths,
    query_weight,
    key_weight,
    value_weight,
    out_weight,
    up_weight,
    down_weight,
    query_bias,
    value_bias,
    out_bias,
    norm1_gain,
    norm1_shift,
    up_bias,
    down_bias,
    norm2_gain,
    norm2_shift,
):
    rows, width = tokens.shape
    groups = lax.axis_size("tensor")
    position = lax.axis_index("tensor")
    head_cols = width // groups
    hidden_cols = FF // groups
    slot_len = lengths[0]
    col_start = position * head_cols
    hid_start = position * hidden_cols
    part = rows // CHUNKS
    cut = [slice(c * part, (c + 1) * part) for c in range(CHUNKS)]
    every = range(CHUNKS)
    run = part // 2
    limits = jnp.stack(
        [
            slot_len - ((position ^ p) * rows + c * part + side * run)
            for c in range(CHUNKS)
            for p, side in half_order()
        ]
    ).astype(jnp.int32)
    row_live = (position * rows + jnp.arange(rows, dtype=jnp.int32) < slot_len).astype(jnp.float32)[
        :, None
    ]
    bias_query = lax.dynamic_slice_in_dim(query_bias, col_start, head_cols)
    bias_value = lax.dynamic_slice_in_dim(value_bias, col_start, head_cols)
    bias_up = lax.dynamic_slice_in_dim(up_bias, hid_start, hidden_cols)
    bias_proj = jnp.concatenate([bias_query, jnp.zeros_like(bias_query), bias_value])

    proj_full = gather_weight(jnp.concatenate([query_weight, key_weight, value_weight], axis=1))
    out_full = gather_weight(out_weight)
    up_full = gather_weight(up_weight)
    down_full = gather_weight(down_weight)


    def lists(count):
        return ([None] * CHUNKS for _ in range(count))

    near, far, seq_tokens, projected = lists(4)
    before = ()
    for c in every:
        near[c] = gather_near(tokens[cut[c]], *before)
        far[c] = gather_far(near[c])
        before = far[c] or near[c]
        seq_tokens[c] = gathered(
            tokens[cut[c]], near[c], together(far[c], *projected[:c]) if far[c] else []
        )
        projected[c] = low(nn(seq_tokens[c], proj_full) + bias_proj)

    context, lse, attn_low = lists(3)
    context[0], lse[0] = attend(0, projected, limits, run)
    attn_low[0] = low(nt(context[0], out_full))
    near[0] = scatter_near(attn_low[0])
    context[1], lse[1] = attend(1, [after(p, attn_low[0]) for p in projected], limits, run)
    far[0] = scatter_far(near[0], context[1])
    attn_low[1] = low(nt(after(context[1], *near[0][1]), out_full))

    def first_norm(c):
        attn_sum = scattered(near[c], far[c])
        result = norm_rows(wide(tokens[cut[c]]) + attn_sum + out_bias, norm1_gain, norm1_shift)
        return (*result, low(result[0]))

    def second_norm(c):
        ffn_sum = scattered(near[c], far[c])
        final, unit2, inverse2 = norm_rows(mid[c] + ffn_sum + down_bias, norm2_gain, norm2_shift)
        grad_final = wide(cotangent[cut[c]]) * row_live[cut[c]]
        grad_sum, gain_part, shift_part = norm_back(grad_final, unit2, inverse2, norm2_gain)
        return (
            low(final * row_live[cut[c]]),
            grad_sum,
            (gain_part, shift_part, jnp.sum(grad_sum, axis=0)),
            low(grad_sum),
        )

    def first_norm_back(c):
        mid_sum = scattered(near[c], far[c])
        grad_sum, gain_part, shift_part = norm_back(
            grad_sum2[c] + mid_sum, unit1[c], inverse1[c], norm1_gain
        )
        return (grad_sum, (gain_part, shift_part, jnp.sum(grad_sum, axis=0)), low(grad_sum))

    def turn(terms, norm):
        near[1] = scatter_near(terms, *far[0])
        results = [norm(0), None]
        out = results[0][-1]
        far[1], near[0] = scatter_far_gather_near(near[1], out)
        results[1] = norm(1)
        far[0] = gather_far(near[0])
        whole = gathered(out, near[0], far[0])
        near[1] = gather_near(results[1][-1], *(far[0] or near[0]))
        return results, after(whole, results[1][-1])

    results, source = turn(attn_low[1], first_norm)
    mid, unit1, inverse1, mid_out = zip(*results)
    mid_seq, activ, slope, ffn_low = lists(4)
    mid_seq[0] = source
    activ[0], slope[0] = gate_and_slope(nn(source, up_full) + bias_up)
    far[1] = gather_far(near[1])
    ffn_low[0] = low(nt(after(activ[0], *near[1]), down_full))
    mid_seq[1] = gathered(mid_out[1], near[1], far[1])
    near[0] = scatter_near(ffn_low[0], *(far[1] or near[1]))
    activ[1], slope[1] = gate_and_slope(nn(after(mid_seq[1], ffn_low[0]), up_full) + bias_up)
    far[0] = scatter_far(near[0])
    ffn_low[1] = low(nt(after(activ[1], *near[0][1]), down_full))

    results, source = turn(ffn_low[1], second_norm)
    layer_out, grad_sum2, vec2, grad_out2 = zip(*results)
    grad_ffn, grad_pre, mid_low = lists(3)
    grad_ffn[0] = source
    grad_pre[0] = low(nn(source, down_full) * wide(slope[0]))
    far[1] = gather_far(near[1])
    mid_low[0] = low(nt(after(grad_pre[0], *near[1]), up_full))
    grad_ffn[1] = gathered(grad_out2[1], near[1], far[1])
    grad_sum1, vec1, grad_out1, grad_attn, grad_query, attn_near, attn_far = lists(7)
    down_terms, up_terms = lists(2)
    near[0] = scatter_near(mid_low[0], *(far[1] or near[1]))
    down_terms[1] = tn(after(grad_ffn[1], mid_low[0]), activ[1])
    far[0] = scatter_far(near[0])
    down_terms[0] = tn(after(grad_ffn[0], down_terms[1], *near[0][1]), activ[0])
    down_grad = low(add_up(down_terms[::-1]))
    down_part = scatter_weight(after(down_grad, *far[0]))
    grad_sum1[0], vec1[0], grad_out1[0] = first_norm_back(0)
    attn_near[0] = gather_near(grad_out1[0], *far[0])
    grad_pre[1] = low(
        nn(after(grad_ffn[1], down_grad, grad_out1[0]), down_full) * wide(slope[1])
    )
    attn_far[0] = gather_far(attn_near[0])
    mid_low[1] = low(nt(after(grad_pre[1], *attn_near[0]), up_full))
    grad_attn[0] = gathered(grad_out1[0], attn_near[0], attn_far[0])
    near[1] = scatter_near(mid_low[1], *(attn_far[0] or attn_near[0]))
    up_terms[0] = tn(
        after(mid_seq[0], mid_low[1], *(attn_far[0] or attn_near[0])), grad_pre[0]
    )
    far[1] = scatter_far(near[1])
    up_terms[1] = tn(after(mid_seq[1], up_terms[0], *near[1][1]), grad_pre[1])
    up_grad = low(add_up(up_terms))
    up_part = scatter_weight(after(up_grad, *far[1]))
    up_bias_part = add_up([jnp.sum(wide(grad_pre[c]), axis=0) for c in every])
    grad_sum1[1], vec1[1], grad_out1[1] = first_norm_back(1)
    attn_near[1] = gather_near(grad_out1[1], *far[1])
    grad_context = low(nn(after(grad_attn[0], up_grad, grad_out1[1]), out_full))
    grad_query[0], *carry = attend_back(
        0, projected, context[0], grad_context, lse[0], limits, run, None
    )
    attn_far[1] = gather_far(attn_near[1])
    out_term = tn(after(grad_attn[0], grad_query[0], *attn_near[1]), context[0])
    grad_attn[1] = gathered(
        grad_out1[1], attn_near[1], together(attn_far[1], out_term) if attn_far[1] else []
    )
    out_grad = low(out_term + tn(grad_attn[1], context[1]))
    out_part = scatter_weight(out_grad)
    grad_context = low(nn(after(grad_attn[1], out_grad), out_full))
    grad_query[1], *carry = attend_back(
        1, projected, context[1], grad_context, lse[1], limits, run, carry
    )
    size = part * groups
    grad_proj = [
        jnp.concatenate([grad_query[c]] + [a[c * size : (c + 1) * size] for a in carry], axis=1)
        for c in every
    ]
    tokens_low, tokens_grad = lists(2)

    proj_terms = [None] * CHUNKS
    proj_terms[0] = tn(after(seq_tokens[0], down_part), grad_proj[0])
    tokens_low[0] = low(nt(after(grad_proj[0], proj_terms[0]), proj_full))
    near[0] = scatter_near(tokens_low[0])
    proj_terms[1] = tn(after(seq_tokens[1], tokens_low[0]), grad_proj[1])
    proj_grad = low(add_up(proj_terms))
    proj_part = scatter_weight(after(proj_grad, *near[0][1]))
    tokens_low[1] = low(nt(after(grad_proj[1], proj_grad, *near[0][1]), proj_full))
    far[0] = scatter_far(near[0])
    near[1] = scatter_near(tokens_low[1], *(far[0] or near[0][1]))
    proj_bias = add_up(
        [jnp.sum(wide(after(grad_proj[c], tokens_low[1])), axis=0) for c in every]
    )
    sums = total_of(
        [after(add_up([vec2[c][i] for c in every]), up_part, *far[0]) for i in range(3)]
        + [add_up([vec1[c][i] for c in every]) for i in range(3)]
        + [
            placed(up_bias_part, hid_start, FF),
            placed(proj_bias[:head_cols], col_start, width),
            placed(proj_bias[2 * head_cols :], col_start, width),
        ]
    )
    out_part = after(out_part, up_part)
    far[1] = scatter_far(near[1], sums[0])
    for c in every:
        tokens_grad[c] = low(grad_sum1[c] + scattered(near[c], far[c]))
    proj_part, out_part, up_part, down_part = map(wide, (proj_part, out_part, up_part, down_part))
    (
        norm2_gain_grad,
        norm2_shift_grad,
        down_bias_grad,
        norm1_gain_grad,
        norm1_shift_grad,
        out_bias_grad,
        up_bias_grad,
        query_bias_grad,
        value_bias_grad,
    ) = sums
    return (
        jnp.concatenate(layer_out, axis=0),
        jnp.concatenate(tokens_grad, axis=0),
        proj_part[:, :head_cols],
        proj_part[:, head_cols : 2 * head_cols],
        proj_part[:, 2 * head_cols :],
        out_part,
        up_part,
        down_part,
        query_bias_grad,
        value_bias_grad,
        out_bias_grad,
        norm1_gain_grad,
        norm1_shift_grad,
        up_bias_grad,
        down_bias_grad,
        norm2_gain_grad,
        norm2_shift_grad,
    )


def solution(mesh):
    row = P(("dp", "tensor"), None)
    block = P("dp", "tensor")
    share = P(("dp", "tensor"))
    return jax.shard_map(
        per_device,
        mesh=mesh,
        in_specs=(row, row, P("dp")) + (block,) * 6 + (P(),) * 9,
        out_specs=(row, row) + (block,) * 6 + (share,) * 9,
        check_vma=False,
    )
```
